32 devices in a mesh: strike: 8 (over z, core), cross: 4 (over y, x).
Axes of the slice: x: 2, y: 2, z: 4, core: 2. Of those that a mesh axis runs over, the one named last changes fastest.
Arguments:
- velocity: float32 [3, 128, 64, 256], P(None, 'strike', 'cross'), may hold values from -4 to 4
- stress: float32 [6, 128, 64, 256], P(None, 'strike', 'cross'), may hold values from -1.6 to 1.6
- buoyancy: float32 [128, 64, 256], P('strike', 'cross'), may hold values from 0.5 to 1
- lame: float32 [128, 64, 256], P('strike', 'cross'), may hold values from 0.5 to 1.2
- shear: float32 [128, 64, 256], P('strike', 'cross'), may hold values from 0.5 to 1
- fault_tile: int32 [8], replicated, may hold values from 1 to 3
- prestress: float32 [128, 256], P('strike', 'cross'), may hold values from 1.2 to 2.4
- normal_stress: float32 [128, 256], P('strike', 'cross'), may hold values from 2 to 4
- rate_a: float32 [128, 256], P('strike', 'cross'), may hold values from 0.02 to 0.04
- state: float32 [128, 256], P('strike', 'cross'), may hold values from 0.45 to 0.6
Outputs:
- velocity_out: float32 [3, 128, 64, 256], P(None, 'strike', 'cross')
- stress_out: float32 [6, 128, 64, 256], P(None, 'strike', 'cross')
- slip_rate: float32 [128, 256], P('strike', 'cross')
- state_out: float32 [128, 256], P('strike', 'cross')
The draws below stay inside these ranges and needn't reach their ends.
Inputs may be any that keep to these rules, and one draw needn't show every extreme that they name: `fault_tile`: each strike index has its fault plane in the first row of one cross tile other than the first.
All inputs are finite; a program needn't handle non-finite values.
Results may differ from the reference program's by a relative error of at most 0.0003.
Values sent between devices are 32-bit elements; how exact they have to be, the bound alone decides.
No kernel may reach another device: no remote copies, remote signals or barrier semaphores. Data moves between devices by JAX's collectives and lax.ppermute only.
A program may use at most 64 MiB of HBM per device.

```python
import math
import jax
import jax.numpy as jnp

CX = 16
CY = 16
NZ = 256
STEPS = 4
NEWTON = 8
NX = 128
NY = 64
N_STRIKE = 8
N_CROSS = 4


def touch_ends(array, own_key, low, largest):
    index_at = [jax.random.randint(jax.random.fold_in(own_key, axis), (), 0, length) for axis, length in enumerate(array.shape)]
    widest = array.shape.index(max(array.shape))
    neighbour = index_at[:widest] + [(index_at[widest] + 1) % array.shape[widest]] + index_at[widest + 1:]
    return array.at[tuple(index_at)].set(low).at[tuple(neighbour)].set(largest)


def levels(stream_key, extent, split, least, top_value):
    def one(dim, blocks):
        steps = jax.random.uniform(jax.random.fold_in(jax.random.fold_in(stream_key, 6), dim), (blocks,), jnp.float32, least / len(split), top_value / len(split))
        return jnp.repeat(jnp.exp(steps), extent[dim] // blocks).reshape((-1,) + (1,) * (len(extent) - dim - 1))

    gain = one(*split[0])
    for cut in split[1:]:
        gain = gain * one(*cut)
    return gain


def noise(own_key, dims, scale, most, shards=(), held_as=jnp.bfloat16):
    entries = scale * jax.random.normal(own_key, dims, jnp.float32)
    if shards:
        entries = entries * levels(own_key, dims, shards, -0.22, 0.18)
    return jnp.clip(entries, -most, most).astype(held_as)


def setup_inputs(seed: int = 0) -> dict:
    key_list = jax.random.split(jax.random.key(seed), 11)
    velocity = noise(key_list[0], (3, NX, NY, NZ), 0.5, 4.0, ((1, 8), (2, 4)), jnp.float32)
    stress = noise(key_list[1], (6, NX, NY, NZ), 0.2, 1.6, ((1, 8), (2, 4)), jnp.float32)
    buoyancy = jnp.clip(0.5 + 0.5 * jax.random.uniform(key_list[2], (NX, NY, NZ), jnp.float32) ** levels(key_list[2], (NX, NY, NZ), ((0, 8), (1, 4)), -0.2, 0.2), 0.5, 1.0)
    lame = jnp.clip(0.5 + 0.70000005 * jax.random.uniform(key_list[3], (NX, NY, NZ), jnp.float32) ** levels(key_list[3], (NX, NY, NZ), ((0, 8), (1, 4)), -0.2, 0.2), 0.5, 1.2)
    shear = jnp.clip(0.5 + 0.5 * jax.random.uniform(key_list[4], (NX, NY, NZ), jnp.float32) ** levels(key_list[4], (NX, NY, NZ), ((0, 8), (1, 4)), -0.2, 0.2), 0.5, 1.0)
    fault_tile = touch_ends(jax.random.randint(key_list[5], (N_STRIKE,), 1, N_CROSS), jax.random.fold_in(key_list[5], 1), 1, N_CROSS - 1).astype(jnp.int32)
    prestress = jnp.clip(1.2 + 1.2 * jax.random.uniform(key_list[6], (NX, NZ), jnp.float32) ** levels(key_list[6], (NX, NZ), ((0, 8), (1, 4)), -0.2, 0.2), 1.2, 2.4)
    normal_stress = jnp.clip(jnp.exp(math.log(4.0) - 0.6931472 * jax.random.uniform(key_list[7], (NX, NZ), jnp.float32) ** levels(key_list[7], (NX, NZ), ((0, 8), (1, 4)), -0.2, 0.2)), 2.0, 4.0)
    rate_a = jnp.clip(jnp.exp(math.log(0.04) - 0.6931472 * jax.random.uniform(key_list[8], (NX, NZ), jnp.float32) ** levels(key_list[8], (NX, NZ), ((0, 8), (1, 4)), -0.2, 0.2)), 0.02, 0.04)
    state = jnp.clip(0.45 + 0.15000004 * jax.random.uniform(key_list[9], (NX, NZ), jnp.float32) ** levels(key_list[9], (NX, NZ), ((0, 8), (1, 4)), -0.2, 0.2), 0.45, 0.6)
    return dict(velocity=velocity, stress=stress, buoyancy=buoyancy, lame=lame, shear=shear, fault_tile=fault_tile, prestress=prestress, normal_stress=normal_stress, rate_a=rate_a, state=state)


step_ratio = 0.25
ref_rate = 0.001
evolve_rate = 1e-05
base_friction = 0.6
evolve_b = 0.03

def inverse_sinh(value):
    magnitude = jnp.abs(value)
    return jnp.sign(value) * jnp.log(magnitude + jnp.sqrt(magnitude * magnitude + 1.0))

def shifted(field, axis_pos, offset):
    parts = [slice(2, field.shape[position] - 2) for position in range(3)]
    parts[axis_pos] = slice(2 + offset, field.shape[axis_pos] - 2 + offset)
    return field[tuple(parts)]

def forward_diff(field, axis_pos):
    return 1.125 * (shifted(field, axis_pos, 1) - shifted(field, axis_pos, 0)) - (shifted(field, axis_pos, 2) - shifted(field, axis_pos, -1)) / 24.0

def backward_diff(field, axis_pos):
    return 1.125 * (shifted(field, axis_pos, 0) - shifted(field, axis_pos, -1)) - (shifted(field, axis_pos, 1) - shifted(field, axis_pos, -2)) / 24.0

def velocity_update(velocity, padded, buoyancy):
    strike_force = forward_diff(padded[0], 0) + backward_diff(padded[3], 1) + backward_diff(padded[4], 2)
    cross_force = backward_diff(padded[3], 0) + forward_diff(padded[1], 1) + backward_diff(padded[5], 2)
    depth_force = backward_diff(padded[4], 0) + backward_diff(padded[5], 1) + forward_diff(padded[2], 2)
    return velocity + step_ratio * buoyancy * jnp.stack([strike_force, cross_force, depth_force])

def stress_update(stress, padded, lame, shear):
    stretch_strike = backward_diff(padded[0], 0)
    stretch_cross = backward_diff(padded[1], 1)
    stretch_depth = backward_diff(padded[2], 2)
    dilation = stretch_strike + stretch_cross + stretch_depth
    normal = jnp.stack([lame * dilation + 2.0 * shear * stretch_strike, lame * dilation + 2.0 * shear * stretch_cross, lame * dilation + 2.0 * shear * stretch_depth])
    tangent = shear * jnp.stack([forward_diff(padded[0], 1) + forward_diff(padded[1], 0), forward_diff(padded[0], 2) + forward_diff(padded[2], 0), forward_diff(padded[1], 2) + forward_diff(padded[2], 1)])
    return stress + step_ratio * jnp.concatenate([normal, tangent], 0)

def friction(trial, damping, prestress, normal_stress, rate_a, state):
    total = trial + prestress
    width = 2.0 * ref_rate * jnp.exp(-state / rate_a)
    strength = rate_a * normal_stress
    scaled = inverse_sinh(total / (damping * width))
    for iteration in range(NEWTON):
        residual = strength * scaled + damping * width * jnp.sinh(scaled) - total
        slope = strength + damping * width * jnp.cosh(scaled)
        scaled = scaled - residual / slope
    slip = width * jnp.sinh(scaled)
    traction = total - damping * slip
    evolved = state + evolve_rate * (jnp.exp((base_friction - state) / evolve_b) - jnp.abs(slip) / ref_rate)
    return (traction - prestress, slip, evolved)

def pad_all(field):
    return jnp.pad(field, ((0, 0), (2, 2), (2, 2), (2, 2)))

def reference(velocity, stress, buoyancy, lame, shear, fault_tile, prestress, normal_stress, rate_a, state):
    columns = jnp.arange(NX, dtype=jnp.int32)
    planes = (fault_tile[columns // CX] * CY).astype(jnp.int32)
    damping = 0.5 * jnp.sqrt(shear[columns, planes, :] / buoyancy[columns, planes, :])
    slip = jnp.zeros((NX, NZ), jnp.float32)
    for iteration in range(STEPS):
        velocity = velocity_update(velocity, pad_all(stress), buoyancy)
        stress = stress_update(stress, pad_all(velocity), lame, shear)
        trial = stress[3, columns, planes, :]
        change, slip, state = friction(trial, damping, prestress, normal_stress, rate_a, state)
        stress = stress.at[3, columns, planes, :].set(change)
    return (velocity, stress, slip, state)
```

```python
import jax
import jax.numpy as jnp
from jax import lax
from jax.experimental import pallas as pl
from jax.experimental.pallas import tpu as pltpu
from jax.sharding import PartitionSpec as P

STEPS = 4
NEWTON = 8

step_ratio = 0.25
ref_rate = 0.001
evolve_rate = 1e-05
base_friction = 0.6
evolve_b = 0.03
near_weight = 27.0
unit = step_ratio / 24.0

VMEM = pl.BlockSpec(memory_space=pltpu.VMEM)
SMEM = pl.BlockSpec(memory_space=pltpu.SMEM)
PARAMS = pltpu.CompilerParams(vmem_limit_bytes=16 * 1024 * 1024)

STRESS_FACE = (((3, "b"), (4, "b"), (0, "f")), ((3, "b"), (5, "b"), (1, "f")))
VELOCITY_FACE = (((0, "b"), (1, "f"), (2, "f")), ((1, "b"), (0, "f"), (2, "f")))


def layers(kind):
    return (2, 1) if kind == "b" else (1, 2)


def combine(hi, lo, far_hi, far_lo):
    def sub(a, b):
        if a is None:
            return None if b is None else -b
        return a if b is None else a - b

    near, far = sub(hi, lo), sub(far_hi, far_lo)
    if near is None:
        return -far
    near = near_weight * near
    return near if far is None else near - far


def difference(kind, get):
    if kind == "b":
        return combine(get(0), get(-1), get(1), get(-2))
    return combine(get(1), get(0), get(2), get(-1))


def plane_shift(field, axis):
    length = field.shape[axis]
    place = lax.broadcasted_iota(jnp.int32, field.shape, axis)

    def get(k):
        if k == 0:
            return field
        rolled = pltpu.roll(field, (-k) % length, axis)
        keep = place < length - k if k > 0 else place >= -k
        return jnp.where(keep, rolled, 0.0)

    return get


def strike_shift(ref, comp, i, count):
    def get(k):
        return ref[comp, i + k] if 0 <= i + k < count else None

    return get


def add(*terms):
    return sum(terms[1:], terms[0])


def velocity_body(v_ref, s_ref, b_ref, out_ref):
    count = v_ref.shape[1]
    for i in range(count):
        gain = b_ref[i] * unit
        sxx, syy, szz, sxy, sxz, syz = (s_ref[c, i] for c in range(6))
        sxy_y, sxz_z = plane_shift(sxy, 0), plane_shift(sxz, 1)
        force = add(
            difference("f", strike_shift(s_ref, 0, i, count)),
            difference("b", sxy_y),
            difference("b", sxz_z),
        )
        out_ref[0, i] = v_ref[0, i] + gain * force
        force = add(
            difference("b", strike_shift(s_ref, 3, i, count)),
            difference("f", plane_shift(syy, 0)),
            difference("b", plane_shift(syz, 1)),
        )
        out_ref[1, i] = v_ref[1, i] + gain * force
        force = add(
            difference("b", strike_shift(s_ref, 4, i, count)),
            difference("b", plane_shift(syz, 0)),
            difference("f", plane_shift(szz, 1)),
        )
        out_ref[2, i] = v_ref[2, i] + gain * force


def stress_body(s_ref, v_ref, lame_ref, shear_ref, out_ref):
    count = s_ref.shape[1]
    for i in range(count):
        lam, mu = lame_ref[i] * unit, shear_ref[i] * unit
        vx, vy, vz = (v_ref[c, i] for c in range(3))
        ex = difference("b", strike_shift(v_ref, 0, i, count))
        ey = difference("b", plane_shift(vy, 0))
        ez = difference("b", plane_shift(vz, 1))
        spread = lam * (ex + ey + ez)
        twice = 2.0 * mu
        out_ref[0, i] = s_ref[0, i] + (spread + twice * ex)
        out_ref[1, i] = s_ref[1, i] + (spread + twice * ey)
        out_ref[2, i] = s_ref[2, i] + (spread + twice * ez)
        out_ref[3, i] = s_ref[3, i] + mu * (
            difference("f", plane_shift(vx, 0)) + difference("f", strike_shift(v_ref, 1, i, count))
        )
        out_ref[4, i] = s_ref[4, i] + mu * (
            difference("f", plane_shift(vx, 1)) + difference("f", strike_shift(v_ref, 2, i, count))
        )
        out_ref[5, i] = s_ref[5, i] + mu * (
            difference("f", plane_shift(vy, 1)) + difference("f", plane_shift(vz, 0))
        )


def row(axis, comp, i):
    return (comp, i) if axis == 0 else (comp, slice(None), i)


def mat(axis, i):
    return (i,) if axis == 0 else (slice(None), i)


def side(axis):
    name = ("strike", "cross")[axis]
    pos, size = lax.axis_index(name), lax.axis_size(name)
    return lax.rem(pos, 2) == 0, pos > 0, pos < size - 1


def pack(ref, axis, spec, a_ref, b_ref):
    even, _, _ = side(axis)
    count = ref.shape[1 + axis]
    up, down = [], []
    for comp, kind in spec:
        before, after = layers(kind)
        up += [row(axis, comp, count - before + k) for k in range(before)]
        down += [row(axis, comp, k) for k in range(after)]
    for k in range(a_ref.shape[0]):
        high = ref[up[min(k, len(up) - 1)]]
        low = ref[down[min(k, len(down) - 1)]]
        a_ref[k] = lax.select(even, high, low)
        b_ref[k] = lax.select(even, low, high)


def halo_terms(axis, spec, count, a_ref, b_ref):
    even, has_before, has_after = side(axis)
    terms = []
    at_before, at_after = 0, 0
    for comp, kind in spec:
        before, after = layers(kind)
        head, tail = [], []
        for k in range(before):
            j = at_before + k
            value = lax.select(even, b_ref[j], a_ref[j])
            head.append(lax.select(has_before, value, jnp.zeros_like(value)))
        for k in range(after):
            j = at_after + k
            value = lax.select(even, a_ref[j], b_ref[j])
            tail.append(lax.select(has_after, value, jnp.zeros_like(value)))
        at_before, at_after = at_before + before, at_after + after
        if kind == "b":
            update = {0: head[0] - near_weight * head[1], 1: head[1], count - 1: -tail[0]}
        else:
            update = {0: head[0], count - 2: -tail[0], count - 1: near_weight * tail[0] - tail[1]}
        terms.append(update)
    return terms


def velocity_edge_body(v_ref, b_ref, xa, xb, ya, yb, out_ref, *packs):
    for axis, a_ref, b_ref2 in ((0, xa, xb), (1, ya, yb)):
        count = v_ref.shape[1 + axis]
        terms = halo_terms(axis, STRESS_FACE[axis], count, a_ref, b_ref2)
        targets = (1, 2, 0) if axis == 0 else (0, 2, 1)
        for target, update in zip(targets, terms):
            for i, value in update.items():
                at = row(axis, target, i)
                out_ref[at] = out_ref[at] + (b_ref[mat(axis, i)] * unit) * value
    if packs:
        for axis in (0, 1):
            pack(out_ref, axis, VELOCITY_FACE[axis], *packs[2 * axis : 2 * axis + 2])


def inverse_sinh(value):
    magnitude = jnp.abs(value)
    grown = jnp.log(magnitude + jnp.sqrt(magnitude * magnitude + 1.0))
    return jnp.where(value < 0.0, -grown, grown)


def friction(trial, damping, prestress, normal_stress, rate_a, state):
    total = trial + prestress
    width = 2.0 * ref_rate * jnp.exp(-state / rate_a)
    strength = rate_a * normal_stress
    drag = damping * width
    scaled = inverse_sinh(total / drag)
    for iteration in range(NEWTON):
        grow, decay = 0.5 * jnp.exp(scaled), 0.5 * jnp.exp(-scaled)
        residual = strength * scaled + drag * (grow - decay) - total
        slope = strength + drag * (grow + decay)
        scaled = scaled - residual / slope
    slip = width * (0.5 * jnp.exp(scaled) - 0.5 * jnp.exp(-scaled))
    traction = total - damping * slip
    evolved = state + evolve_rate * (
        jnp.exp((base_friction - state) / evolve_b) - jnp.abs(slip) / ref_rate
    )
    return (traction - prestress, slip, evolved)


def stress_edge_body(
    tile_ref, s_ref, lame_ref, shear_ref, b_ref, fault_ref, state_ref, xa, xb, ya, yb,
    out_ref, slip_ref, evolved_ref, *packs
):
    for axis, a_ref, b_ref2 in ((0, xa, xb), (1, ya, yb)):
        count = s_ref.shape[1 + axis]
        terms = halo_terms(axis, VELOCITY_FACE[axis], count, a_ref, b_ref2)
        for i, value in terms[0].items():
            lam, mu = lame_ref[mat(axis, i)] * unit, shear_ref[mat(axis, i)] * unit
            spread = lam * value
            for comp in range(3):
                at = row(axis, comp, i)
                more = spread + 2.0 * mu * value if comp == axis else spread
                out_ref[at] = out_ref[at] + more
        targets = (3, 4) if axis == 0 else (3, 5)
        for target, update in zip(targets, terms[1:]):
            for i, value in update.items():
                at = row(axis, target, i)
                out_ref[at] = out_ref[at] + (shear_ref[mat(axis, i)] * unit) * value
    is_owner = tile_ref[lax.axis_index("strike")] == lax.axis_index("cross")
    first = row(1, 3, 0)
    trial = out_ref[first]
    damping = 0.5 * jnp.sqrt(shear_ref[:, 0] / b_ref[:, 0])
    change, slip, evolved = friction(
        trial, damping, fault_ref[0], fault_ref[1], fault_ref[2], state_ref[...]
    )
    out_ref[first] = lax.select(is_owner, change, trial)
    slip_ref[...] = slip
    evolved_ref[...] = evolved
    if packs:
        for axis in (0, 1):
            pack(out_ref, axis, STRESS_FACE[axis], *packs[2 * axis : 2 * axis + 2])


def pack_body(s_ref, *packs):
    for axis in (0, 1):
        pack(s_ref, axis, STRESS_FACE[axis], *packs[2 * axis : 2 * axis + 2])


def swaps(pairs):
    return [p for i, j in pairs for p in ((i, j), (j, i))]


def exchange_pairs(n_strike, n_cross):
    def at(s, c):
        return s * n_cross + c

    strike_a = [(at(s, c), at(s + 1, c)) for s in range(0, n_strike - 1, 2) for c in range(n_cross)]
    strike_b = [(at(s, c), at(s + 1, c)) for s in range(1, n_strike - 1, 2) for c in range(n_cross)]
    cross_a = [(at(s, c), at(s, c + 1)) for s in range(n_strike) for c in range(0, n_cross - 1, 2)]
    cross_b = [(at(s, c), at(s, c + 1)) for s in range(n_strike) for c in range(1, n_cross - 1, 2)]
    half = n_cross // 2
    for s in (0, n_strike - 1):
        strike_b += [(at(s, c), at(s, c + half)) for c in range(half)]
    for c in (0, n_cross - 1):
        cross_b += [(at(s, c), at(s + 1, c)) for s in range(0, n_strike - 1, 2)]
    return tuple(swaps(p) for p in (strike_a, strike_b, cross_a, cross_b))


def local(
    velocity, stress, buoyancy, lame, shear, fault_tile, prestress, normal_stress, rate_a, state
):
    n_strike, n_cross = lax.axis_size("strike"), lax.axis_size("cross")
    axes = ("strike", "cross")
    strike_pos, cross_pos = lax.axis_index("strike"), lax.axis_index("cross")
    strike_a, strike_b, cross_a, cross_b = exchange_pairs(n_strike, n_cross)
    _, nx, ny, nz = velocity.shape
    bz = prestress.shape[1]
    f32 = jnp.float32
    thick = 5
    vec = lambda *shape: jax.ShapeDtypeStruct(shape, f32)
    faces = (vec(thick, ny, nz), vec(thick, ny, nz), vec(thick, nx, nz), vec(thick, nx, nz))
    like_v, like_s = vec(*velocity.shape), vec(*stress.shape)
    plane = vec(nx, nz)

    def call(body, ins, outs, alias=None, smem=0, name=None):
        return pl.pallas_call(
            body,
            in_specs=[SMEM] * smem + [VMEM] * (len(ins) - smem),
            out_specs=[VMEM] * len(outs),
            out_shape=list(outs),
            input_output_aliases={} if alias is None else {alias: 0},
            compiler_params=PARAMS,
            name=name,
        )(*ins)

    def exchange(packs):
        xa, xb, ya, yb = packs
        yb = lax.ppermute(yb, axes, cross_b)
        ya = lax.ppermute(ya, axes, cross_a)
        xb = lax.ppermute(xb, axes, strike_b)
        xa = lax.ppermute(xa, axes, strike_a)
        return xa, xb, ya, yb

    def partner(block, r):
        pairs = [(s * n_cross + c, s * n_cross + (c ^ r)) for s in range(n_strike) for c in range(n_cross)]
        return lax.ppermute(block, axes, pairs)

    packs = call(pack_body, (stress,), faces, name="pack")
    own = jnp.concatenate([prestress, normal_stress, rate_a, state], axis=1)
    blocks = jnp.stack([own] + [partner(own, r) for r in range(1, n_cross)])
    blocks = jnp.take(blocks, jnp.arange(n_cross) ^ cross_pos, axis=0)
    fault = blocks.reshape(n_cross, nx, 4, bz).transpose(2, 1, 0, 3).reshape(4, nx, nz)
    fault_state = fault[3]

    for iteration in range(STEPS):
        halos = exchange(packs)
        (velocity,) = call(velocity_body, (velocity, stress, buoyancy), (like_v,), 0, name="velocity")
        velocity, *packs = call(
            velocity_edge_body, (velocity, buoyancy, *halos), (like_v, *faces), 0, name="velocity_edge"
        )
        halos = exchange(packs)
        (stress,) = call(stress_body, (stress, velocity, lame, shear), (like_s,), 0, name="stress")
        outs = (like_s, plane, plane) + (faces if iteration < STEPS - 1 else ())
        stress, slip, fault_state, *packs = call(
            stress_edge_body,
            (fault_tile, stress, lame, shear, buoyancy, fault, fault_state, *halos),
            outs, 1, smem=1, name="stress_edge",
        )

    both = jnp.stack([slip, fault_state])
    owner = fault_tile[strike_pos]
    result = jnp.zeros((2, nx, bz), f32)
    for r in range(n_cross):
        target = cross_pos ^ r
        part = lax.dynamic_slice_in_dim(both, target * bz, bz, axis=2)
        got = part if r == 0 else partner(part, r)
        result = jnp.where(owner == target, got, result)
    return (velocity, stress, result[0], result[1])


def solution(mesh):
    in_specs = (
        P(None, "strike", "cross", None),
        P(None, "strike", "cross", None),
        P("strike", "cross", None),
        P("strike", "cross", None),
        P("strike", "cross", None),
        P(),
        P("strike", "cross"),
        P("strike", "cross"),
        P("strike", "cross"),
        P("strike", "cross"),
    )
    out_specs = (
        P(None, "strike", "cross", None),
        P(None, "strike", "cross", None),
        P("strike", "cross"),
        P("strike", "cross"),
    )
    return jax.shard_map(local, mesh=mesh, in_specs=in_specs, out_specs=out_specs, check_vma=False)
```

```python
import jax
import jax.numpy as jnp
from jax import lax
from jax.experimental import pallas as pl
from jax.experimental.pallas import tpu as pltpu
from jax.sharding import PartitionSpec as P


STEPS = 4
NEWTON = 8

step_ratio = 0.25
ref_rate = 0.001
evolve_rate = 1e-05
base_friction = 0.6
evolve_b = 0.03
near_weight = 27.0
unit = step_ratio / 24.0

VMEM = pl.BlockSpec(memory_space=pltpu.VMEM)
SMEM = pl.BlockSpec(memory_space=pltpu.SMEM)
HBM = pl.BlockSpec(memory_space=pltpu.HBM)
PARAMS = pltpu.CompilerParams(vmem_limit_bytes=16 * 1024 * 1024)

STRESS_FACE = (((3, "b"), (4, "b"), (0, "f")), ((3, "b"), (5, "b"), (1, "f")))
VELOCITY_FACE = (((0, "b"), (1, "f"), (2, "f")), ((1, "b"), (0, "f"), (2, "f")))


def layers(kind):
    return (2, 1) if kind == "b" else (1, 2)


def combine(hi, lo, far_hi, far_lo):
    def sub(a, b):
        if a is None:
            return None if b is None else -b
        return a if b is None else a - b

    near, far = sub(hi, lo), sub(far_hi, far_lo)
    if near is None:
        return -far
    near = near_weight * near
    return near if far is None else near - far


def difference(kind, get):
    if kind == "b":
        return combine(get(0), get(-1), get(1), get(-2))
    return combine(get(1), get(0), get(2), get(-1))


def plane_shift(field, axis):
    length = field.shape[axis]
    place = lax.broadcasted_iota(jnp.int32, field.shape, axis)

    def get(k):
        if k == 0:
            return field
        rolled = pltpu.roll(field, (-k) % length, axis)
        keep = place < length - k if k > 0 else place >= -k
        return jnp.where(keep, rolled, 0.0)

    return get


def strike_shift(ref, comp, i, count):
    def get(k):
        return ref[comp, i + k] if 0 <= i + k < count else None

    return get


def add(*terms):
    return sum(terms[1:], terms[0])


def velocity_body(v_ref, s_ref, b_ref, out_ref):
    count = v_ref.shape[1]
    for i in range(count):
        gain = b_ref[i] * unit
        _, syy, szz, sxy, sxz, syz = (s_ref[c, i] for c in range(6))
        sxy_y, sxz_z = plane_shift(sxy, 0), plane_shift(sxz, 1)
        force = add(
            difference("f", strike_shift(s_ref, 0, i, count)),
            difference("b", sxy_y),
            difference("b", sxz_z),
        )
        out_ref[0, i] = v_ref[0, i] + gain * force
        force = add(
            difference("b", strike_shift(s_ref, 3, i, count)),
            difference("f", plane_shift(syy, 0)),
            difference("b", plane_shift(syz, 1)),
        )
        out_ref[1, i] = v_ref[1, i] + gain * force
        force = add(
            difference("b", strike_shift(s_ref, 4, i, count)),
            difference("b", plane_shift(syz, 0)),
            difference("f", plane_shift(szz, 1)),
        )
        out_ref[2, i] = v_ref[2, i] + gain * force


def stress_store_body(s_ref, v_ref, lame_ref, shear_ref, out_ref, store_ref, sem):
    copy = pltpu.make_async_copy(v_ref, store_ref, sem)
    copy.start()
    stress_body(s_ref, v_ref, lame_ref, shear_ref, out_ref)
    copy.wait()


def stress_body(s_ref, v_ref, lame_ref, shear_ref, out_ref):
    count = s_ref.shape[1]
    for i in range(count):
        lam, mu = lame_ref[i] * unit, shear_ref[i] * unit
        vx, vy, vz = (v_ref[c, i] for c in range(3))
        ex = difference("b", strike_shift(v_ref, 0, i, count))
        ey = difference("b", plane_shift(vy, 0))
        ez = difference("b", plane_shift(vz, 1))
        spread = lam * (ex + ey + ez)
        twice = 2.0 * mu
        out_ref[0, i] = s_ref[0, i] + (spread + twice * ex)
        out_ref[1, i] = s_ref[1, i] + (spread + twice * ey)
        out_ref[2, i] = s_ref[2, i] + (spread + twice * ez)
        out_ref[3, i] = s_ref[3, i] + mu * (
            difference("f", plane_shift(vx, 0)) + difference("f", strike_shift(v_ref, 1, i, count))
        )
        out_ref[4, i] = s_ref[4, i] + mu * (
            difference("f", plane_shift(vx, 1)) + difference("f", strike_shift(v_ref, 2, i, count))
        )
        out_ref[5, i] = s_ref[5, i] + mu * (
            difference("f", plane_shift(vy, 1)) + difference("f", plane_shift(vz, 0))
        )


def row(axis, comp, i):
    return (comp, i) if axis == 0 else (comp, slice(None), i)


def mat(axis, i):
    return (i,) if axis == 0 else (slice(None), i)


def side(axis):
    name = ("strike", "cross")[axis]
    pos, size = lax.axis_index(name), lax.axis_size(name)
    return lax.rem(pos, 2) == 0, pos > 0, pos < size - 1


def pack(ref, axis, spec, a_ref, b_ref):
    even, _, _ = side(axis)
    count = ref.shape[1 + axis]
    up, down = [], []
    for comp, kind in spec:
        before, after = layers(kind)
        up += [row(axis, comp, count - before + k) for k in range(before)]
        down += [row(axis, comp, k) for k in range(after)]
    for k in range(a_ref.shape[0]):
        high = ref[up[min(k, len(up) - 1)]]
        low = ref[down[min(k, len(down) - 1)]]
        a_ref[k] = lax.select(even, high, low)
        b_ref[k] = lax.select(even, low, high)


def halo_terms(axis, spec, count, a_ref, b_ref):
    even, has_before, has_after = side(axis)
    terms = []
    at_before, at_after = 0, 0
    for comp, kind in spec:
        before, after = layers(kind)
        head, tail = [], []
        for k in range(before):
            j = at_before + k
            value = lax.select(even, b_ref[j], a_ref[j])
            head.append(lax.select(has_before, value, jnp.zeros_like(value)))
        for k in range(after):
            j = at_after + k
            value = lax.select(even, a_ref[j], b_ref[j])
            tail.append(lax.select(has_after, value, jnp.zeros_like(value)))
        at_before, at_after = at_before + before, at_after + after
        if kind == "b":
            update = {0: head[0] - near_weight * head[1], 1: head[1], count - 1: -tail[0]}
        else:
            update = {0: head[0], count - 2: -tail[0], count - 1: near_weight * tail[0] - tail[1]}
        terms.append(update)
    return terms


def velocity_edge_body(v_ref, b_ref, xa, xb, ya, yb, out_ref, *packs):
    for axis, a_ref, b_ref2 in ((0, xa, xb), (1, ya, yb)):
        count = v_ref.shape[1 + axis]
        terms = halo_terms(axis, STRESS_FACE[axis], count, a_ref, b_ref2)
        targets = (1, 2, 0) if axis == 0 else (0, 2, 1)
        for target, update in zip(targets, terms):
            for i, value in update.items():
                at = row(axis, target, i)
                out_ref[at] = out_ref[at] + (b_ref[mat(axis, i)] * unit) * value
    if packs:
        for axis in (0, 1):
            pack(out_ref, axis, VELOCITY_FACE[axis], *packs[2 * axis : 2 * axis + 2])


def inverse_sinh(value):
    magnitude = jnp.abs(value)
    grown = jnp.log(magnitude + jnp.sqrt(magnitude * magnitude + 1.0))
    return jnp.where(value < 0.0, -grown, grown)


def friction(trial, damping, prestress, normal_stress, rate_a, state):
    total = trial + prestress
    width = 2.0 * ref_rate * jnp.exp(-state / rate_a)
    strength = rate_a * normal_stress
    drag = damping * width
    scaled = inverse_sinh(total / drag)
    for _ in range(NEWTON):
        grow, decay = 0.5 * jnp.exp(scaled), 0.5 * jnp.exp(-scaled)
        residual = strength * scaled + drag * (grow - decay) - total
        slope = strength + drag * (grow + decay)
        scaled = scaled - residual / slope
    slip = width * (0.5 * jnp.exp(scaled) - 0.5 * jnp.exp(-scaled))
    traction = total - damping * slip
    evolved = state + evolve_rate * (
        jnp.exp((base_friction - state) / evolve_b) - jnp.abs(slip) / ref_rate
    )
    return (traction - prestress, slip, evolved)


def stress_edge_body(
    tile_ref, s_ref, lame_ref, shear_ref, b_ref, load_ref, normal_ref, rate_ref, state_ref, xa, xb, ya, yb,
    out_ref, *rest
):
    for axis, a_ref, b_ref2 in ((0, xa, xb), (1, ya, yb)):
        count = s_ref.shape[1 + axis]
        terms = halo_terms(axis, VELOCITY_FACE[axis], count, a_ref, b_ref2)
        for i, value in terms[0].items():
            lam, mu = lame_ref[mat(axis, i)] * unit, shear_ref[mat(axis, i)] * unit
            spread = lam * value
            for comp in range(3):
                at = row(axis, comp, i)
                more = spread + 2.0 * mu * value if comp == axis else spread
                out_ref[at] = out_ref[at] + more
        targets = (3, 4) if axis == 0 else (3, 5)
        for target, update in zip(targets, terms[1:]):
            for i, value in update.items():
                at = row(axis, target, i)
                out_ref[at] = out_ref[at] + (shear_ref[mat(axis, i)] * unit) * value
    is_owner = tile_ref[lax.axis_index("strike")] == lax.axis_index("cross")
    first = row(1, 3, 0)
    trial = out_ref[first]
    damping = 0.5 * jnp.sqrt(shear_ref[:, 0] / b_ref[:, 0])
    change, slip, evolved = friction(
        trial, damping, load_ref[...], normal_ref[...], rate_ref[...], state_ref[...]
    )
    out_ref[first] = lax.select(is_owner, change, trial)
    if len(rest[-1].shape) == 3:
        evolved_ref, *packs = rest
        evolved_ref[...] = evolved
        for axis in (0, 1):
            pack(out_ref, axis, STRESS_FACE[axis], *packs[2 * axis : 2 * axis + 2])
    else:
        spread_out(slip, evolved, rest)


def spread_out(slip, evolved, sends):
    lanes = sends[0].shape[1]
    width, rows = slip.shape[1], lanes // 2
    place = lax.broadcasted_iota(jnp.int32, slip.shape, 1)
    me = lax.axis_index("cross")
    for r, send_ref in enumerate(sends):
        offset = (me ^ r) * rows
        head = pltpu.roll(slip, lax.rem(width - offset, width), 1)
        tail = pltpu.roll(evolved, lax.rem(width + rows - offset, width), 1)
        send_ref[...] = jnp.where(place < rows, head, tail)[:, :lanes]


def finish_body(tile_ref, send_ref, *refs):
    *got, slip_ref, state_ref = refs
    owner = tile_ref[lax.axis_index("strike")]
    me = lax.axis_index("cross")
    value = send_ref[...]
    for r, ref in enumerate(got, 1):
        value = lax.select(owner == (me ^ r), ref[...], value)
    rows = slip_ref.shape[1]
    slip_ref[...] = value[:, :rows]
    state_ref[...] = pltpu.roll(value, rows, 1)[:, :rows]


def own_body(*refs):
    *parts, out_ref = refs
    pieces = [ref[...] for ref in parts]
    rest = out_ref.shape[1] - sum(p.shape[1] for p in pieces)
    if rest:
        pieces.append(jnp.zeros((out_ref.shape[0], rest), out_ref.dtype))
    out_ref[...] = jnp.concatenate(pieces, axis=1)


def fault_body(*refs):
    arrays = 4
    blocks, outs = refs[:-arrays], refs[-arrays:]
    count, width = len(blocks), blocks[0].shape[1]
    depth = outs[0].shape[1]
    rows = depth // count
    me = lax.axis_index("cross")
    held = [ref[...] for ref in blocks]
    place = lax.broadcasted_iota(jnp.int32, held[0].shape, 1)
    whole = [jnp.zeros_like(held[0])] * arrays
    for q in range(count):
        value = held[0]
        for r in range(1, count):
            value = lax.select((me ^ r) == q, held[r], value)
        mine = (place >= q * rows) & (place < (q + 1) * rows)
        for k in range(arrays):
            shift = ((q - k) * rows) % width
            moved = pltpu.roll(value, shift, 1) if shift else value
            whole[k] = jnp.where(mine, moved, whole[k])
    for out_ref, value in zip(outs, whole):
        out_ref[...] = value[:, :depth]


def pack_body(s_ref, *packs):
    for axis in (0, 1):
        pack(s_ref, axis, STRESS_FACE[axis], *packs[2 * axis : 2 * axis + 2])


def swaps(pairs):
    return [p for i, j in pairs for p in ((i, j), (j, i))]


def exchange_pairs(n_strike, n_cross):
    def at(s, c):
        return s * n_cross + c

    strike_a = [(at(s, c), at(s + 1, c)) for s in range(0, n_strike - 1, 2) for c in range(n_cross)]
    strike_b = [(at(s, c), at(s + 1, c)) for s in range(1, n_strike - 1, 2) for c in range(n_cross)]
    cross_a = [(at(s, c), at(s, c + 1)) for s in range(n_strike) for c in range(0, n_cross - 1, 2)]
    cross_b = [(at(s, c), at(s, c + 1)) for s in range(n_strike) for c in range(1, n_cross - 1, 2)]
    half = n_cross // 2
    for s in (0, n_strike - 1):
        strike_b += [(at(s, c), at(s, c + half)) for c in range(half)]
    for c in (0, n_cross - 1):
        cross_b += [(at(s, c), at(s + 1, c)) for s in range(0, n_strike - 1, 2)]
    return tuple(swaps(p) for p in (strike_a, strike_b, cross_a, cross_b))


def local(
    velocity, stress, buoyancy, lame, shear, fault_tile, prestress, normal_stress, rate_a, state
):
    n_strike, n_cross = lax.axis_size("strike"), lax.axis_size("cross")
    axes = ("strike", "cross")
    strike_a, strike_b, cross_a, cross_b = exchange_pairs(n_strike, n_cross)
    _, nx, ny, nz = velocity.shape
    bz = prestress.shape[1]
    f32 = jnp.float32
    thick = 5
    vec = lambda *shape: jax.ShapeDtypeStruct(shape, f32)
    faces = (vec(thick, ny, nz), vec(thick, ny, nz), vec(thick, nx, nz), vec(thick, nx, nz))
    like_v, like_s = pltpu.VMEM(velocity.shape, f32), pltpu.VMEM(stress.shape, f32)
    plane = vec(nx, nz)

    def call(body, ins, outs, specs=None, alias=None, scratch=()):
        return pl.pallas_call(
            body,
            in_specs=[VMEM] * len(ins) if specs is None else specs,
            out_specs=[HBM if getattr(o, "hbm", False) else VMEM for o in outs],
            out_shape=[o.shape if getattr(o, "hbm", False) else o for o in outs],
            input_output_aliases={} if alias is None else {alias: 0},
            compiler_params=PARAMS,
            scratch_shapes=scratch,
        )(*ins)

    def exchange(packs):
        perms = dict(xa=strike_a, xb=strike_b, ya=cross_a, yb=cross_b)
        halos = {}
        for name, block in reversed(tuple(zip(perms, packs))):
            halos[name] = lax.ppermute(block, axes, perms[name])
        return [halos[name] for name in perms]

    def partner(block, r):
        pairs = [(s * n_cross + c, s * n_cross + (c ^ r)) for s in range(n_strike) for c in range(n_cross)]
        return lax.ppermute(block, axes, pairs)

    width = max(nz, 4 * bz)
    (own,) = call(own_body, (prestress, normal_stress, rate_a, state), (vec(nx, width),))
    packs = call(pack_body, (stress,), faces)
    for iteration in range(STEPS):
        first, last = iteration == 0, iteration == STEPS - 1
        halos = exchange(packs)
        if first:
            blocks = [own] + [partner(own, r) for r in range(1, n_cross)]
            *fault, fault_state = call(fault_body, blocks, (plane,) * 4)
        (velocity,) = call(
            velocity_body, (velocity, stress, buoyancy), (like_v,),
            alias=None if first else 0,
        )
        velocity, *packs = call(
            velocity_edge_body, (velocity, buoyancy, *halos), (like_v, *faces), alias=0,
        )
        halos = exchange(packs)
        body, outs, scratch = stress_body, (like_s,), ()
        if last:
            body, outs = stress_store_body, (like_s, Stored(vec(*velocity.shape)))
            scratch = [pltpu.SemaphoreType.DMA]
        stress, *stored = call(
            body, (stress, velocity, lame, shear), outs,
            alias=None if first else 0, scratch=scratch,
        )
        outs = (like_s,) + (vec(nx, 2 * bz),) * n_cross if last else (like_s, plane, *faces)
        stress, fault_state, *packs = call(
            stress_edge_body,
            (fault_tile, stress, lame, shear, buoyancy, *fault, fault_state, *halos),
            outs, [SMEM] + [VMEM] * 12, alias=1,
        )

    sends = [fault_state, *packs]
    got = [partner(sends[r], r) for r in range(1, n_cross)]
    slip_out, state_out = call(
        finish_body, (fault_tile, sends[0], *got), (vec(nx, bz), vec(nx, bz)),
        [SMEM] + [VMEM] * n_cross,
    )
    return (stored[0], stress, slip_out, state_out)


class Stored:
    hbm = True

    def __init__(self, shape):
        self.shape = shape


def solution(mesh):
    in_specs = (
        P(None, "strike", "cross", None),
        P(None, "strike", "cross", None),
        P("strike", "cross", None),
        P("strike", "cross", None),
        P("strike", "cross", None),
        P(),
        P("strike", "cross"),
        P("strike", "cross"),
        P("strike", "cross"),
        P("strike", "cross"),
    )
    out_specs = (
        P(None, "strike", "cross", None),
        P(None, "strike", "cross", None),
        P("strike", "cross"),
        P("strike", "cross"),
    )
    return jax.shard_map(local, mesh=mesh, in_specs=in_specs, out_specs=out_specs, check_vma=False)
```

```python
import jax
import jax.numpy as jnp
from jax import lax
from jax.experimental import pallas as pl
from jax.experimental.pallas import tpu as pltpu
from jax.sharding import PartitionSpec as P


STEPS = 4
NEWTON = 8

step_ratio = 0.25
ref_rate = 0.001
evolve_rate = 1e-05
base_friction = 0.6
evolve_b = 0.03
near_weight = 27.0
unit = step_ratio / 24.0

VMEM = pl.BlockSpec(memory_space=pltpu.VMEM)
SMEM = pl.BlockSpec(memory_space=pltpu.SMEM)
HBM = pl.BlockSpec(memory_space=pltpu.HBM)
PARAMS = pltpu.CompilerParams(vmem_limit_bytes=16 * 1024 * 1024)

STRESS_FACE = (((3, "b"), (4, "b"), (0, "f")), ((3, "b"), (5, "b"), (1, "f")))
VELOCITY_FACE = (((0, "b"), (1, "f"), (2, "f")), ((1, "b"), (0, "f"), (2, "f")))


def layers(kind):
    return (2, 1) if kind == "b" else (1, 2)


def combine(hi, lo, far_hi, far_lo):
    def sub(a, b):
        if a is None:
            return None if b is None else -b
        return a if b is None else a - b

    near, far = sub(hi, lo), sub(far_hi, far_lo)
    if near is None:
        return -far
    near = near_weight * near
    return near if far is None else near - far


def difference(kind, get):
    if kind == "b":
        return combine(get(0), get(-1), get(1), get(-2))
    return combine(get(1), get(0), get(2), get(-1))


def plane_shift(field, axis):
    length = field.shape[axis]
    place = lax.broadcasted_iota(jnp.int32, field.shape, axis)

    def get(k):
        if k == 0:
            return field
        rolled = pltpu.roll(field, (-k) % length, axis)
        keep = place < length - k if k > 0 else place >= -k
        return jnp.where(keep, rolled, 0.0)

    return get


def strike_shift(ref, comp, i, count):
    def get(k):
        return ref[comp, i + k] if 0 <= i + k < count else None

    return get


def add(*terms):
    return sum(terms[1:], terms[0])


def velocity_load_body(v_ref, s_ref, b_ref, out_ref, sem):
    groups = sem.shape[0]
    size = v_ref.shape[1] // groups
    copies = []
    for g in range(groups):
        part = (slice(None), pl.ds(g * size, size))
        copies.append(pltpu.make_async_copy(v_ref.at[part], out_ref.at[part], sem.at[g]))
        copies[g].start()

    def before(i):
        if i % size == 0:
            copies[i // size].wait()

    velocity_body(out_ref, s_ref, b_ref, out_ref, before)


def velocity_body(v_ref, s_ref, b_ref, out_ref, before=None):
    count = v_ref.shape[1]
    for i in range(count):
        if before is not None:
            before(i)
        gain = b_ref[i] * unit
        _, syy, szz, sxy, sxz, syz = (s_ref[c, i] for c in range(6))
        sxy_y, sxz_z = plane_shift(sxy, 0), plane_shift(sxz, 1)
        force = add(
            difference("f", strike_shift(s_ref, 0, i, count)),
            difference("b", sxy_y),
            difference("b", sxz_z),
        )
        out_ref[0, i] = v_ref[0, i] + gain * force
        force = add(
            difference("b", strike_shift(s_ref, 3, i, count)),
            difference("f", plane_shift(syy, 0)),
            difference("b", plane_shift(syz, 1)),
        )
        out_ref[1, i] = v_ref[1, i] + gain * force
        force = add(
            difference("b", strike_shift(s_ref, 4, i, count)),
            difference("b", plane_shift(syz, 0)),
            difference("f", plane_shift(szz, 1)),
        )
        out_ref[2, i] = v_ref[2, i] + gain * force


def stress_store_body(s_ref, v_ref, lame_ref, shear_ref, out_ref, store_ref, sem):
    copy = pltpu.make_async_copy(v_ref, store_ref, sem)
    copy.start()
    stress_body(s_ref, v_ref, lame_ref, shear_ref, out_ref)
    copy.wait()


def stress_body(s_ref, v_ref, lame_ref, shear_ref, out_ref):
    count = s_ref.shape[1]
    for i in range(count):
        lam, mu = lame_ref[i] * unit, shear_ref[i] * unit
        vx, vy, vz = (v_ref[c, i] for c in range(3))
        ex = difference("b", strike_shift(v_ref, 0, i, count))
        ey = difference("b", plane_shift(vy, 0))
        ez = difference("b", plane_shift(vz, 1))
        spread = lam * (ex + ey + ez)
        twice = 2.0 * mu
        out_ref[0, i] = s_ref[0, i] + (spread + twice * ex)
        out_ref[1, i] = s_ref[1, i] + (spread + twice * ey)
        out_ref[2, i] = s_ref[2, i] + (spread + twice * ez)
        out_ref[3, i] = s_ref[3, i] + mu * (
            difference("f", plane_shift(vx, 0)) + difference("f", strike_shift(v_ref, 1, i, count))
        )
        out_ref[4, i] = s_ref[4, i] + mu * (
            difference("f", plane_shift(vx, 1)) + difference("f", strike_shift(v_ref, 2, i, count))
        )
        out_ref[5, i] = s_ref[5, i] + mu * (
            difference("f", plane_shift(vy, 1)) + difference("f", plane_shift(vz, 0))
        )


def row(axis, comp, i):
    return (comp, i) if axis == 0 else (comp, slice(None), i)


def mat(axis, i):
    return (i,) if axis == 0 else (slice(None), i)


def side(axis):
    name = ("strike", "cross")[axis]
    pos, size = lax.axis_index(name), lax.axis_size(name)
    return lax.rem(pos, 2) == 0, pos > 0, pos < size - 1


def pack(ref, axis, spec, a_ref, b_ref):
    even, _, _ = side(axis)
    count = ref.shape[1 + axis]
    up, down = [], []
    for comp, kind in spec:
        before, after = layers(kind)
        up += [row(axis, comp, count - before + k) for k in range(before)]
        down += [row(axis, comp, k) for k in range(after)]
    for k in range(max(len(up), len(down))):
        high = ref[up[min(k, len(up) - 1)]]
        low = ref[down[min(k, len(down) - 1)]]
        a_ref[k] = lax.select(even, high, low)
        b_ref[k] = lax.select(even, low, high)


def halo_terms(axis, spec, count, a_ref, b_ref):
    even, has_before, has_after = side(axis)
    terms = []
    at_before, at_after = 0, 0
    for comp, kind in spec:
        before, after = layers(kind)
        head, tail = [], []
        for k in range(before):
            j = at_before + k
            value = lax.select(even, b_ref[j], a_ref[j])
            head.append(lax.select(has_before, value, jnp.zeros_like(value)))
        for k in range(after):
            j = at_after + k
            value = lax.select(even, a_ref[j], b_ref[j])
            tail.append(lax.select(has_after, value, jnp.zeros_like(value)))
        at_before, at_after = at_before + before, at_after + after
        if kind == "b":
            update = {0: head[0] - near_weight * head[1], 1: head[1], count - 1: -tail[0]}
        else:
            update = {0: head[0], count - 2: -tail[0], count - 1: near_weight * tail[0] - tail[1]}
        terms.append(update)
    return terms


def velocity_edge_body(v_ref, b_ref, xa, xb, ya, yb, out_ref, *packs):
    for axis, a_ref, b_ref2 in ((0, xa, xb), (1, ya, yb)):
        count = v_ref.shape[1 + axis]
        terms = halo_terms(axis, STRESS_FACE[axis], count, a_ref, b_ref2)
        targets = (1, 2, 0) if axis == 0 else (0, 2, 1)
        for target, update in zip(targets, terms):
            for i, value in update.items():
                at = row(axis, target, i)
                out_ref[at] = out_ref[at] + (b_ref[mat(axis, i)] * unit) * value
    for axis in (0, 1):
        pack(out_ref, axis, VELOCITY_FACE[axis], *packs[2 * axis : 2 * axis + 2])


def velocity_ride_body(own_ref, v_ref, b_ref, xa, xb, ya, yb, out_ref, *packs):
    velocity_edge_body(v_ref, b_ref, xa, xb, ya, yb, out_ref, *packs)
    last = packs[3].shape[0] - 1
    packs[3][last - 1] = own_ref[...]
    packs[3][last] = ya[ya.shape[0] - 1]


def inverse_sinh(value):
    magnitude = jnp.abs(value)
    grown = jnp.log(magnitude + jnp.sqrt(magnitude * magnitude + 1.0))
    return jnp.where(value < 0.0, -grown, grown)


def friction(trial, damping, prestress, normal_stress, rate_a, state):
    total = trial + prestress
    width = 2.0 * ref_rate * jnp.exp(-state / rate_a)
    strength = rate_a * normal_stress
    drag = damping * width
    scaled = inverse_sinh(total / drag)
    for _ in range(NEWTON):
        grow, decay = 0.5 * jnp.exp(scaled), 0.5 * jnp.exp(-scaled)
        residual = strength * scaled + drag * (grow - decay) - total
        slope = strength + drag * (grow + decay)
        scaled = scaled - residual / slope
    slip = width * (0.5 * jnp.exp(scaled) - 0.5 * jnp.exp(-scaled))
    traction = total - damping * slip
    evolved = state + evolve_rate * (
        jnp.exp((base_friction - state) / evolve_b) - jnp.abs(slip) / ref_rate
    )
    return (traction - prestress, slip, evolved)


def stress_edge_body(
    owner_ref, s_ref, lame_ref, shear_ref, b_ref, load_ref, normal_ref, rate_ref, state_ref, xa, xb, ya, yb,
    out_ref, *rest
):
    for axis, a_ref, b_ref2 in ((0, xa, xb), (1, ya, yb)):
        count = s_ref.shape[1 + axis]
        terms = halo_terms(axis, VELOCITY_FACE[axis], count, a_ref, b_ref2)
        for i, value in terms[0].items():
            lam, mu = lame_ref[mat(axis, i)] * unit, shear_ref[mat(axis, i)] * unit
            spread = lam * value
            for comp in range(3):
                at = row(axis, comp, i)
                more = spread + 2.0 * mu * value if comp == axis else spread
                out_ref[at] = out_ref[at] + more
        targets = (3, 4) if axis == 0 else (3, 5)
        for target, update in zip(targets, terms[1:]):
            for i, value in update.items():
                at = row(axis, target, i)
                out_ref[at] = out_ref[at] + (shear_ref[mat(axis, i)] * unit) * value
    is_owner = owner_ref[...] > 0.5
    first = row(1, 3, 0)
    trial = out_ref[first]
    damping = 0.5 * jnp.sqrt(shear_ref[:, 0] / b_ref[:, 0])
    change, slip, evolved = friction(
        trial, damping, load_ref[...], normal_ref[...], rate_ref[...], state_ref[...]
    )
    out_ref[first] = jnp.where(is_owner, change, trial)
    if len(rest[-1].shape) == 3:
        evolved_ref, *packs = rest
        evolved_ref[...] = evolved
        for axis in (0, 1):
            pack(out_ref, axis, STRESS_FACE[axis], *packs[2 * axis : 2 * axis + 2])
    else:
        spread_out(jnp.where(is_owner, slip, 0.0), jnp.where(is_owner, evolved, 0.0), rest)


def spread_out(slip, evolved, sends):
    lanes = sends[0].shape[1]
    width, rows = slip.shape[1], lanes // 2
    place = lax.broadcasted_iota(jnp.int32, slip.shape, 1)
    me = lax.axis_index("cross")
    for r, send_ref in enumerate(sends):
        offset = (me ^ r) * rows
        head = pltpu.roll(slip, lax.rem(width - offset, width), 1)
        tail = pltpu.roll(evolved, lax.rem(width + rows - offset, width), 1)
        send_ref[...] = jnp.where(place < rows, head, tail)[:, :lanes]


def owner_body(tile_ref, owner_ref):
    mine = tile_ref[lax.axis_index("strike")] == lax.axis_index("cross")
    owner_ref[...] = jnp.full(owner_ref.shape, mine.astype(jnp.float32))


def join(pieces, width):
    rest = width - sum(p.shape[1] for p in pieces)
    if rest:
        pieces.append(jnp.zeros((pieces[0].shape[0], rest), pieces[0].dtype))
    return jnp.concatenate(pieces, axis=1)


def fault_body(order, *refs):
    arrays = 4
    blocks, outs = refs[:-arrays], refs[-arrays:]
    held = [block[...] for block in blocks]
    count, width = len(held), held[0].shape[1]
    depth = outs[0].shape[1]
    rows = depth // count
    holder = order(lax.axis_index("cross"))
    place = lax.broadcasted_iota(jnp.int32, held[0].shape, 1)
    whole = [jnp.zeros_like(held[0])] * arrays
    for q in range(count):
        value = held[0]
        for at, block in zip(holder[1:], held[1:]):
            value = lax.select(at == q, block, value)
        mine = (place >= q * rows) & (place < (q + 1) * rows)
        for k in range(arrays):
            shift = ((q - k) * rows) % width
            moved = pltpu.roll(value, shift, 1) if shift else value
            whole[k] = jnp.where(mine, moved, whole[k])
    for out_ref, value in zip(outs, whole):
        out_ref[...] = value[:, :depth]


def pack_body(s_ref, *rest):
    *sources, s_out, xa, xb, ya, yb, own_ref, part_ref, s_sem, part_sem = rest
    copies = [pltpu.make_async_copy(ref, part_ref.at[k], part_sem.at[k]) for k, ref in enumerate(sources)]
    copies += [pltpu.make_async_copy(s_ref.at[c], s_out.at[c], s_sem.at[c]) for c in range(s_ref.shape[0])]
    for copy in copies:
        copy.start()
    for copy in copies:
        copy.wait()
    own = join([part_ref[k] for k in range(len(sources))], own_ref.shape[1])
    own_ref[...] = own
    for axis, a_ref, b_ref in ((0, xa, xb), (1, ya, yb)):
        pack(s_out, axis, STRESS_FACE[axis], a_ref, b_ref)
    if ya.shape[0] > yb.shape[0]:
        ya[ya.shape[0] - 1] = own


def swaps(pairs):
    return [p for i, j in pairs for p in ((i, j), (j, i))]


def exchange_pairs(n_strike, n_cross):
    def at(s, c):
        return s * n_cross + c

    strike_a = [(at(s, c), at(s + 1, c)) for s in range(0, n_strike - 1, 2) for c in range(n_cross)]
    strike_b = [(at(s, c), at(s + 1, c)) for s in range(1, n_strike - 1, 2) for c in range(n_cross)]
    cross_a = [(at(s, c), at(s, c + 1)) for s in range(n_strike) for c in range(0, n_cross - 1, 2)]
    cross_b = [(at(s, c), at(s, c + 1)) for s in range(n_strike) for c in range(1, n_cross - 1, 2)]
    cross_ring = cross_b + [(at(s, 0), at(s, n_cross - 1)) for s in range(n_strike)]
    half = n_cross // 2
    for s in (0, n_strike - 1):
        strike_b += [(at(s, c), at(s, c + half)) for c in range(half)]
    for c in (0, n_cross - 1):
        cross_b += [(at(s, c), at(s + 1, c)) for s in range(0, n_strike - 1, 2)]
    return tuple(swaps(p) for p in (strike_a, strike_b, cross_a, cross_b, cross_ring))


def cycle_order(me):
    size = lax.axis_size("cross")
    far = lax.rem(me + jnp.where(lax.rem(me, 2) == 0, size - 1, 1), size)
    return [me, me ^ 1, far, far ^ 1]


def local(
    velocity, stress, buoyancy, lame, shear, fault_tile, prestress, normal_stress, rate_a, state
):
    n_strike, n_cross = lax.axis_size("strike"), lax.axis_size("cross")
    axes = ("strike", "cross")
    strike_a, strike_b, cross_a, cross_b, cross_ring = exchange_pairs(n_strike, n_cross)
    _, nx, ny, nz = velocity.shape
    bz = prestress.shape[1]
    f32 = jnp.float32
    thick = 5
    vec = lambda *shape: jax.ShapeDtypeStruct(shape, f32)
    faces = (vec(thick, ny, nz), vec(thick, ny, nz), vec(thick, nx, nz), vec(thick, nx, nz))
    like_v, like_s = pltpu.VMEM(velocity.shape, f32), pltpu.VMEM(stress.shape, f32)
    plane = vec(nx, nz)

    def call(body, ins, outs, specs=None, alias=None, scratch=()):
        return pl.pallas_call(
            body,
            in_specs=[VMEM] * len(ins) if specs is None else specs,
            out_specs=[HBM if getattr(o, "hbm", False) else VMEM for o in outs],
            out_shape=[o.shape if getattr(o, "hbm", False) else o for o in outs],
            input_output_aliases={} if alias is None else {alias: 0},
            compiler_params=PARAMS,
            scratch_shapes=scratch,
        )(*ins)

    def exchange(packs, wrap=False):
        perms = dict(xa=strike_a, xb=strike_b, ya=cross_a, yb=cross_ring if wrap else cross_b)
        halos = {}
        for name, block in reversed(tuple(zip(perms, packs))):
            halos[name] = lax.ppermute(block, axes, perms[name])
        return [halos[name] for name in perms]

    def partner(block, r):
        pairs = [(s * n_cross + c, s * n_cross + (c ^ r)) for s in range(n_strike) for c in range(n_cross)]
        return lax.ppermute(block, axes, pairs)

    ride = n_cross == 4
    width = max(nz, 4 * bz)
    params = (prestress, normal_stress, rate_a, state)
    outs = (like_s, *faces[:2], vec(thick + ride, nx, nz), faces[3], vec(nx, width))
    sources = [pltpu.with_memory_space_constraint(x, pltpu.HBM) for x in (stress, *params)]
    dma = pltpu.SemaphoreType.DMA
    stress, *packs, own = call(
        pack_body, sources, outs, [HBM] * 5,
        scratch=[pltpu.VMEM((4, nx, bz), f32), dma((stress.shape[0],)), dma((4,))],
    )
    for iteration in range(STEPS):
        first, last = iteration == 0, iteration == STEPS - 1
        halos = exchange(packs)
        if first:
            (owner,) = call(owner_body, (fault_tile,), (plane,), [SMEM])
            source = pltpu.with_memory_space_constraint(velocity, pltpu.HBM)
            (velocity,) = call(
                velocity_load_body, (source, stress, buoyancy), (like_v,),
                [HBM, VMEM, VMEM], scratch=[pltpu.SemaphoreType.DMA((4,))],
            )
        else:
            (velocity,) = call(velocity_body, (velocity, stress, buoyancy), (like_v,), alias=0)
        if first and ride:
            velocity, *packs = call(
                velocity_ride_body, (own, velocity, buoyancy, *halos),
                (like_v, *faces[:3], vec(thick + 2, nx, nz)), alias=1,
            )
            near = halos[2]
        else:
            velocity, *packs = call(
                velocity_edge_body, (velocity, buoyancy, *halos), (like_v, *faces), alias=0,
            )
        halos = exchange(packs, wrap=first and ride)
        body, outs, scratch = stress_body, (like_s,), ()
        if last:
            body, outs = stress_store_body, (like_s, Stored(vec(*velocity.shape)))
            scratch = [pltpu.SemaphoreType.DMA]
        stress, *stored = call(
            body, (stress, velocity, lame, shear), outs,
            alias=0, scratch=scratch,
        )
        if first:
            if ride:
                blocks, order = (own, near, halos[3]), cycle_order
                body = lambda own, near, far, *outs: fault_body(
                    order, own, near.at[thick], far.at[thick], far.at[thick + 1], *outs
                )
            else:
                blocks = [own] + [partner(own, r) for r in range(1, n_cross)]
                order = lambda me: [me ^ r for r in range(n_cross)]
                body = lambda *refs: fault_body(order, *refs)
            *fault, fault_state = call(body, blocks, (plane,) * 4)
        outs = (like_s,) + (vec(nx, 2 * bz),) * n_cross if last else (like_s, plane, *faces)
        stress, fault_state, *packs = call(
            stress_edge_body,
            (owner, stress, lame, shear, buoyancy, *fault, fault_state, *halos),
            outs, alias=1,
        )

    sends = [fault_state, *packs]
    result = sum([partner(sends[r], r) for r in range(1, n_cross)], sends[0])
    return (stored[0], stress, result[:, :bz], result[:, bz:])


class Stored:
    hbm = True

    def __init__(self, shape):
        self.shape = shape


def solution(mesh):
    in_specs = (
        P(None, "strike", "cross", None),
        P(None, "strike", "cross", None),
        P("strike", "cross", None),
        P("strike", "cross", None),
        P("strike", "cross", None),
        P(),
        P("strike", "cross"),
        P("strike", "cross"),
        P("strike", "cross"),
        P("strike", "cross"),
    )
    out_specs = (
        P(None, "strike", "cross", None),
        P(None, "strike", "cross", None),
        P("strike", "cross"),
        P("strike", "cross"),
    )
    return jax.shard_map(local, mesh=mesh, in_specs=in_specs, out_specs=out_specs, check_vma=False)
```

```python
import functools

import jax
import jax.numpy as jnp
from jax import lax
from jax.experimental import pallas as pl
from jax.experimental.pallas import tpu as pltpu
from jax.sharding import PartitionSpec as P


STEPS = 4
NEWTON = 8

step_ratio = 0.25
ref_rate = 0.001
evolve_rate = 1e-05
base_friction = 0.6
evolve_b = 0.03
near_weight = 27.0
unit = step_ratio / 24.0

VMEM = pl.BlockSpec(memory_space=pltpu.VMEM)
SMEM = pl.BlockSpec(memory_space=pltpu.SMEM)
HBM = pl.BlockSpec(memory_space=pltpu.HBM)
PARAMS = pltpu.CompilerParams(vmem_limit_bytes=16 * 1024 * 1024)

STRESS_FACE = (((3, "b"), (4, "b"), (0, "f")), ((3, "b"), (5, "b"), (1, "f")))
VELOCITY_FACE = (((0, "b"), (1, "f"), (2, "f")), ((1, "b"), (0, "f"), (2, "f")))


def layers(kind):
    return (2, 1) if kind == "b" else (1, 2)


def combine(hi, lo, far_hi, far_lo):
    def sub(a, b):
        if a is None:
            return None if b is None else -b
        return a if b is None else a - b

    near, far = sub(hi, lo), sub(far_hi, far_lo)
    if near is None:
        return -far
    near = near_weight * near
    return near if far is None else near - far


def difference(kind, get):
    if kind == "b":
        return combine(get(0), get(-1), get(1), get(-2))
    return combine(get(1), get(0), get(2), get(-1))


def plane_shift(field, axis):
    length = field.shape[axis]
    place = lax.broadcasted_iota(jnp.int32, field.shape, axis)

    def get(k):
        if k == 0:
            return field
        rolled = pltpu.roll(field, (-k) % length, axis)
        keep = place < length - k if k > 0 else place >= -k
        return jnp.where(keep, rolled, 0.0)

    return get


def strike_shift(ref, comp, i, count):
    def get(k):
        return ref[comp, i + k] if 0 <= i + k < count else None

    return get


def add(*terms):
    return sum(terms[1:], terms[0])


def velocity_load_body(
    tile_ref, v_ref, s_ref, b_ref, out_ref, owner_ref, rows_ref, first_ref, sem, tile_smem, tile_sem
):
    groups = sem.shape[0]
    size = v_ref.shape[1] // groups
    parts = [(slice(None), pl.ds(g * size, size)) for g in range(groups)]
    copies = [
        pltpu.make_async_copy(v_ref.at[part], first_ref.at[part], sem.at[g])
        for g, part in enumerate(parts)
    ]
    tile_copy = pltpu.make_async_copy(tile_ref, tile_smem, tile_sem)
    for copy in (*copies, tile_copy):
        copy.start()
    for k, value in enumerate(edge_rows(b_ref, unit)):
        rows_ref[k] = value
    velocity_body(None, s_ref, b_ref, out_ref)
    tile_copy.wait()
    mine = tile_smem[lax.axis_index("strike")] == lax.axis_index("cross")
    owner_ref[...] = jnp.full(owner_ref.shape, mine.astype(jnp.float32))
    for copy, part in zip(copies, parts):
        copy.wait()
        out_ref[part] = out_ref[part] + first_ref[part]


def velocity_body(v_ref, s_ref, b_ref, out_ref):
    count = out_ref.shape[1]

    def store(comp, i, more):
        out_ref[comp, i] = more if v_ref is None else v_ref[comp, i] + more

    for i in range(count):
        gain = b_ref[i] * unit
        _, syy, szz, sxy, sxz, syz = (s_ref[c, i] for c in range(6))
        sxy_y, sxz_z = plane_shift(sxy, 0), plane_shift(sxz, 1)
        force = add(
            difference("f", strike_shift(s_ref, 0, i, count)),
            difference("b", sxy_y),
            difference("b", sxz_z),
        )
        store(0, i, gain * force)
        force = add(
            difference("b", strike_shift(s_ref, 3, i, count)),
            difference("f", plane_shift(syy, 0)),
            difference("b", plane_shift(syz, 1)),
        )
        store(1, i, gain * force)
        force = add(
            difference("b", strike_shift(s_ref, 4, i, count)),
            difference("b", plane_shift(syz, 0)),
            difference("f", plane_shift(szz, 1)),
        )
        store(2, i, gain * force)


def stress_store_body(s_ref, v_ref, lame_ref, shear_ref, out_ref, store_ref, sem):
    copy = pltpu.make_async_copy(v_ref, store_ref, sem)
    copy.start()
    stress_body(s_ref, v_ref, lame_ref, shear_ref, out_ref)
    copy.wait()


def stress_body(s_ref, v_ref, lame_ref, shear_ref, out_ref):
    count = s_ref.shape[1]
    for i in range(count):
        lam, mu = lame_ref[i] * unit, shear_ref[i] * unit
        vx, vy, vz = (v_ref[c, i] for c in range(3))
        ex = difference("b", strike_shift(v_ref, 0, i, count))
        ey = difference("b", plane_shift(vy, 0))
        ez = difference("b", plane_shift(vz, 1))
        spread = lam * (ex + ey + ez)
        twice = 2.0 * mu
        out_ref[0, i] = s_ref[0, i] + (spread + twice * ex)
        out_ref[1, i] = s_ref[1, i] + (spread + twice * ey)
        out_ref[2, i] = s_ref[2, i] + (spread + twice * ez)
        out_ref[3, i] = s_ref[3, i] + mu * (
            difference("f", plane_shift(vx, 0)) + difference("f", strike_shift(v_ref, 1, i, count))
        )
        out_ref[4, i] = s_ref[4, i] + mu * (
            difference("f", plane_shift(vx, 1)) + difference("f", strike_shift(v_ref, 2, i, count))
        )
        out_ref[5, i] = s_ref[5, i] + mu * (
            difference("f", plane_shift(vy, 1)) + difference("f", plane_shift(vz, 0))
        )


def row(axis, comp, i):
    return (comp, i) if axis == 0 else (comp, slice(None), i)


def slot(i, count):
    return i if i < 2 else i - count + 4


def edge_rows(ref, scale):
    count = ref.shape[1]
    return [ref[:, i] * scale for i in (0, 1, count - 2, count - 1)]


def side(axis):
    name = ("strike", "cross")[axis]
    pos, size = lax.axis_index(name), lax.axis_size(name)
    return lax.rem(pos, 2) == 0, pos > 0, pos < size - 1


def pack_steps(ref, axis, spec, a_ref, b_ref, rows=None):
    even, _, _ = side(axis)
    count = ref.shape[1 + axis]
    up, down = [], []
    for comp, kind in spec:
        before, after = layers(kind)
        up += [(comp, count - before + k) for k in range(before)]
        down += [(comp, k) for k in range(after)]

    def read(comp, i):
        if rows is not None:
            return rows[comp, i]
        return ref[row(axis, comp, i)]

    def step(k, first, second):
        high, low = read(*first), read(*second)
        a_ref[k] = lax.select(even, high, low)
        b_ref[k] = lax.select(even, low, high)

    for k in range(max(len(up), len(down))):
        first, second = up[min(k, len(up) - 1)], down[min(k, len(down) - 1)]
        yield (first, second), functools.partial(step, k, first, second)


def pack(*args):
    for _, step in pack_steps(*args):
        step()


def halo_terms(axis, spec, count, a_ref, b_ref):
    even, has_before, has_after = side(axis)
    terms = []
    at_before, at_after = 0, 0
    for comp, kind in spec:
        before, after = layers(kind)
        head, tail = [], []
        for k in range(before):
            j = at_before + k
            value = lax.select(even, b_ref[j], a_ref[j])
            head.append(lax.select(has_before, value, jnp.zeros_like(value)))
        for k in range(after):
            j = at_after + k
            value = lax.select(even, a_ref[j], b_ref[j])
            tail.append(lax.select(has_after, value, jnp.zeros_like(value)))
        at_before, at_after = at_before + before, at_after + after
        if kind == "b":
            update = {0: head[0] - near_weight * head[1], 1: head[1], count - 1: -tail[0]}
        else:
            update = {0: head[0], count - 2: -tail[0], count - 1: near_weight * tail[0] - tail[1]}
        terms.append(update)
    return terms


def grow(ref, at, more):
    value = ref[at] + more
    ref[at] = value
    return value


def velocity_edge_body(v_ref, b_ref, b_rows, xa, xb, ya, yb, out_ref, *packs):
    count = v_ref.shape[1]
    terms = halo_terms(0, STRESS_FACE[0], count, xa, xb)
    for target, update in zip((1, 2, 0), terms):
        for i, value in update.items():
            grow(out_ref, row(0, target, i), (b_ref[i] * unit) * value)
    count = v_ref.shape[2]
    terms = halo_terms(1, STRESS_FACE[1], count, ya, yb)
    rows = {}
    for target, update in zip((0, 2, 1), terms):
        for i, value in update.items():
            rows[target, i] = grow(out_ref, row(1, target, i), b_rows[slot(i, count)] * value)
    pack(out_ref, 1, VELOCITY_FACE[1], *packs[2:], rows)
    pack(out_ref, 0, VELOCITY_FACE[0], *packs[:2])


def velocity_ride_body(own_ref, v_ref, b_ref, b_rows, xa, xb, ya, yb, out_ref, *packs):
    velocity_edge_body(v_ref, b_ref, b_rows, xa, xb, ya, yb, out_ref, *packs)
    last = packs[3].shape[0] - 1
    packs[3][last - 1] = own_ref[...]
    packs[3][last] = ya[ya.shape[0] - 1]


def inverse_sinh(value):
    magnitude = jnp.abs(value)
    grown = jnp.log(magnitude + jnp.sqrt(magnitude * magnitude + 1.0))
    return jnp.where(value < 0.0, -grown, grown)


def friction(trial, damping, prestress, normal_stress, rate_a, state):
    total = trial + prestress
    width = 2.0 * ref_rate * jnp.exp(-state / rate_a)
    strength = rate_a * normal_stress
    drag = damping * width
    scaled = inverse_sinh(total / drag)
    yield
    for _ in range(NEWTON):
        grow, decay = 0.5 * jnp.exp(scaled), 0.5 * jnp.exp(-scaled)
        residual = strength * scaled + drag * (grow - decay) - total
        slope = strength + drag * (grow + decay)
        scaled = scaled - residual / slope
        yield
    slip = width * (0.5 * jnp.exp(scaled) - 0.5 * jnp.exp(-scaled))
    traction = total - damping * slip
    evolved = state + evolve_rate * (
        jnp.exp((base_friction - state) / evolve_b) - jnp.abs(slip) / ref_rate
    )
    yield (traction - prestress, slip, evolved)


def stress_edge_body(
    owner_ref, s_ref, lame_ref, shear_ref, material_rows, damping_ref, load_ref, normal_ref,
    rate_ref, state_ref, xa, xb, ya, yb, out_ref, *rest
):
    rows = {}
    counts = s_ref.shape[1:3]
    terms = [
        halo_terms(axis, VELOCITY_FACE[axis], counts[axis], a_ref, b_ref)
        for axis, a_ref, b_ref in ((0, xa, xb), (1, ya, yb))
    ]

    def material(axis, kind, i):
        if axis == 0:
            return (lame_ref, shear_ref)[kind][i] * unit
        return material_rows[4 * kind + slot(i, counts[axis])]

    def correct(axis, comp, i, more):
        value = grow(out_ref, row(axis, comp, i), more)
        if axis == 1:
            rows[comp, i] = value

    def tangent(axis, comp, i, value):
        correct(axis, comp, i, material(axis, 1, i) * value)

    def normal(axis, i, value):
        spread = material(axis, 0, i) * value
        for comp in range(3):
            more = spread + 2.0 * material(axis, 1, i) * value if comp == axis else spread
            correct(axis, comp, i, more)

    for i, value in terms[0][1].items():
        tangent(0, 3, i, value)
    tangent(1, 3, 0, terms[1][1].pop(0))
    trial = rows[3, 0]
    solve = friction(
        trial, damping_ref[...], load_ref[...], normal_ref[...], rate_ref[...], state_ref[...]
    )
    work = [functools.partial(tangent, 1, 3, i, value) for i, value in terms[1][1].items()]
    for axis, comp in ((0, 4), (1, 5)):
        work += [functools.partial(tangent, axis, comp, i, value) for i, value in terms[axis][2].items()]
    for axis in (0, 1):
        work += [functools.partial(normal, axis, i, value) for i, value in terms[axis][0].items()]
    after = []
    packs = rest[1:] if len(rest[-1].shape) == 3 else ()
    if packs:
        for axis, held in ((1, rows), (0, None)):
            for reads, step in pack_steps(
                out_ref, axis, STRESS_FACE[axis], *packs[2 * axis : 2 * axis + 2], held
            ):
                late = any(comp == 3 and (axis == 0 or i == 0) for comp, i in reads)
                (after if late else work).append(step)
    stages = NEWTON + 1
    for stage in range(stages):
        next(solve)
        for step in work[stage * len(work) // stages : (stage + 1) * len(work) // stages]:
            step()
    change, slip, evolved = next(solve)
    is_owner = owner_ref[...] > 0.5
    rows[3, 0] = jnp.where(is_owner, change, trial)
    out_ref[row(1, 3, 0)] = rows[3, 0]
    for step in after:
        step()
    if packs:
        rest[0][...] = evolved
    else:
        spread_out(jnp.where(is_owner, slip, 0.0), jnp.where(is_owner, evolved, 0.0), rest)


def spread_out(slip, evolved, sends):
    lanes = sends[0].shape[1]
    width, rows = slip.shape[1], lanes // 2
    place = lax.broadcasted_iota(jnp.int32, slip.shape, 1)
    me = lax.axis_index("cross")
    for r, send_ref in enumerate(sends):
        offset = (me ^ r) * rows
        head = pltpu.roll(slip, lax.rem(width - offset, width), 1)
        tail = pltpu.roll(evolved, lax.rem(width + rows - offset, width), 1)
        send_ref[...] = jnp.where(place < rows, head, tail)[:, :lanes]


def stress_rows_body(b_ref, lame_ref, shear_ref, rows_ref, damping_ref):
    for k, value in enumerate(edge_rows(lame_ref, unit) + edge_rows(shear_ref, unit)):
        rows_ref[k] = value
    damping_ref[...] = 0.5 * jnp.sqrt(shear_ref[:, 0] / b_ref[:, 0])


def join(pieces, width):
    rest = width - sum(p.shape[1] for p in pieces)
    if rest:
        pieces.append(jnp.zeros((pieces[0].shape[0], rest), pieces[0].dtype))
    return jnp.concatenate(pieces, axis=1)


def fault_body(order, *refs):
    arrays = 4
    blocks, outs = refs[:-arrays], refs[-arrays:]
    held = [block[...] for block in blocks]
    count, width = len(held), held[0].shape[1]
    depth = outs[0].shape[1]
    rows = depth // count
    holder = order(lax.axis_index("cross"))
    place = lax.broadcasted_iota(jnp.int32, held[0].shape, 1)
    whole = [jnp.zeros_like(held[0])] * arrays
    for q in range(count):
        value = held[0]
        for at, block in zip(holder[1:], held[1:]):
            value = lax.select(at == q, block, value)
        mine = (place >= q * rows) & (place < (q + 1) * rows)
        for k in range(arrays):
            shift = ((q - k) * rows) % width
            moved = pltpu.roll(value, shift, 1) if shift else value
            whole[k] = jnp.where(mine, moved, whole[k])
    for out_ref, value in zip(outs, whole):
        out_ref[...] = value[:, :depth]


def pack_body(s_ref, *rest):
    *sources, s_out, xa, xb, ya, yb, own_ref, part_ref, s_sem, part_sem = rest
    copies = [pltpu.make_async_copy(ref, part_ref.at[k], part_sem.at[k]) for k, ref in enumerate(sources)]
    copies += [pltpu.make_async_copy(s_ref.at[c], s_out.at[c], s_sem.at[c]) for c in range(s_ref.shape[0])]
    for copy in copies:
        copy.start()
    for copy in copies:
        copy.wait()
    own = join([part_ref[k] for k in range(len(sources))], own_ref.shape[1])
    own_ref[...] = own
    for axis, a_ref, b_ref in ((0, xa, xb), (1, ya, yb)):
        pack(s_out, axis, STRESS_FACE[axis], a_ref, b_ref)
    if ya.shape[0] > yb.shape[0]:
        ya[ya.shape[0] - 1] = own


def swaps(pairs):
    return [p for i, j in pairs for p in ((i, j), (j, i))]


def exchange_pairs(n_strike, n_cross):
    def at(s, c):
        return s * n_cross + c

    strike_a = [(at(s, c), at(s + 1, c)) for s in range(0, n_strike - 1, 2) for c in range(n_cross)]
    strike_b = [(at(s, c), at(s + 1, c)) for s in range(1, n_strike - 1, 2) for c in range(n_cross)]
    cross_a = [(at(s, c), at(s, c + 1)) for s in range(n_strike) for c in range(0, n_cross - 1, 2)]
    cross_b = [(at(s, c), at(s, c + 1)) for s in range(n_strike) for c in range(1, n_cross - 1, 2)]
    cross_ring = cross_b + [(at(s, 0), at(s, n_cross - 1)) for s in range(n_strike)]
    half = n_cross // 2
    for s in (0, n_strike - 1):
        strike_b += [(at(s, c), at(s, c + half)) for c in range(half)]
    for c in (0, n_cross - 1):
        cross_b += [(at(s, c), at(s + 1, c)) for s in range(0, n_strike - 1, 2)]
    return tuple(swaps(p) for p in (strike_a, strike_b, cross_a, cross_b, cross_ring))


def cycle_order(me):
    size = lax.axis_size("cross")
    far = lax.rem(me + jnp.where(lax.rem(me, 2) == 0, size - 1, 1), size)
    return [me, me ^ 1, far, far ^ 1]


def local(
    velocity, stress, buoyancy, lame, shear, fault_tile, prestress, normal_stress, rate_a, state
):
    n_strike, n_cross = lax.axis_size("strike"), lax.axis_size("cross")
    axes = ("strike", "cross")
    strike_a, strike_b, cross_a, cross_b, cross_ring = exchange_pairs(n_strike, n_cross)
    _, nx, ny, nz = velocity.shape
    bz = prestress.shape[1]
    f32 = jnp.float32
    thick = 5
    vec = lambda *shape: jax.ShapeDtypeStruct(shape, f32)
    faces = (vec(thick, ny, nz), vec(thick, ny, nz), vec(thick, nx, nz), vec(thick, nx, nz))
    like_v, like_s = pltpu.VMEM(velocity.shape, f32), pltpu.VMEM(stress.shape, f32)
    plane = vec(nx, nz)

    def call(body, ins, outs, specs=None, alias=None, scratch=()):
        return pl.pallas_call(
            body,
            in_specs=[VMEM] * len(ins) if specs is None else specs,
            out_specs=[HBM if getattr(o, "hbm", False) else VMEM for o in outs],
            out_shape=[o.shape if getattr(o, "hbm", False) else o for o in outs],
            input_output_aliases={} if alias is None else {alias: 0},
            compiler_params=PARAMS,
            scratch_shapes=scratch,
        )(*ins)

    def exchange(packs, wrap=False):
        perms = dict(xa=strike_a, xb=strike_b, ya=cross_a, yb=cross_ring if wrap else cross_b)
        halos = {}
        for name, block in reversed(tuple(zip(perms, packs))):
            halos[name] = lax.ppermute(block, axes, perms[name])
        return [halos[name] for name in perms]

    def partner(block, r):
        pairs = [(s * n_cross + c, s * n_cross + (c ^ r)) for s in range(n_strike) for c in range(n_cross)]
        return lax.ppermute(block, axes, pairs)

    ride = n_cross == 4
    width = max(nz, 4 * bz)
    params = (prestress, normal_stress, rate_a, state)
    outs = (like_s, *faces[:2], vec(thick + ride, nx, nz), faces[3], vec(nx, width))
    sources = [pltpu.with_memory_space_constraint(x, pltpu.HBM) for x in (stress, *params)]
    dma = pltpu.SemaphoreType.DMA
    stress, *packs, own = call(
        pack_body, sources, outs, [HBM] * 5,
        scratch=[pltpu.VMEM((4, nx, bz), f32), dma((stress.shape[0],)), dma((4,))],
    )
    for iteration in range(STEPS):
        first, last = iteration == 0, iteration == STEPS - 1
        halos = exchange(packs)
        if first:
            sources = [pltpu.with_memory_space_constraint(x, pltpu.HBM) for x in (fault_tile, velocity)]
            velocity, owner, b_rows = call(
                velocity_load_body, (*sources, stress, buoyancy),
                (like_v, plane, vec(4, nx, nz)), [HBM, HBM, VMEM, VMEM],
                scratch=[
                    pltpu.VMEM(velocity.shape, f32), dma((4,)), pltpu.SMEM(fault_tile.shape, jnp.int32), dma
                ],
            )
        else:
            (velocity,) = call(velocity_body, (velocity, stress, buoyancy), (like_v,), alias=0)
        if first and ride:
            velocity, *packs = call(
                velocity_ride_body, (own, velocity, buoyancy, b_rows, *halos),
                (like_v, *faces[:3], vec(thick + 2, nx, nz)), alias=1,
            )
            near = halos[2]
        else:
            velocity, *packs = call(
                velocity_edge_body, (velocity, buoyancy, b_rows, *halos), (like_v, *faces), alias=0,
            )
        halos = exchange(packs, wrap=first and ride)
        if first:
            rows, damping = call(stress_rows_body, (buoyancy, lame, shear), (vec(8, nx, nz), plane))
        body, outs, scratch = stress_body, (like_s,), ()
        if last:
            body, outs = stress_store_body, (like_s, Stored(vec(*velocity.shape)))
            scratch = [pltpu.SemaphoreType.DMA]
        stress, *stored = call(
            body, (stress, velocity, lame, shear), outs,
            alias=0, scratch=scratch,
        )
        if first:
            if ride:
                blocks, order = (own, near, halos[3]), cycle_order
                body = lambda own, near, far, *outs: fault_body(
                    order, own, near.at[thick], far.at[thick], far.at[thick + 1], *outs
                )
            else:
                blocks = [own] + [partner(own, r) for r in range(1, n_cross)]
                order = lambda me: [me ^ r for r in range(n_cross)]
                body = lambda *refs: fault_body(order, *refs)
            *fault, fault_state = call(body, blocks, (plane,) * 4)
        outs = (like_s,) + (vec(nx, 2 * bz),) * n_cross if last else (like_s, plane, *faces)
        stress, fault_state, *packs = call(
            stress_edge_body,
            (owner, stress, lame, shear, rows, damping, *fault, fault_state, *halos),
            outs, alias=1,
        )

    sends = [fault_state, *packs]
    result = sum([partner(sends[r], r) for r in range(1, n_cross)], sends[0])
    return (stored[0], stress, result[:, :bz], result[:, bz:])


class Stored:
    hbm = True

    def __init__(self, shape):
        self.shape = shape


def solution(mesh):
    in_specs = (
        P(None, "strike", "cross", None),
        P(None, "strike", "cross", None),
        P("strike", "cross", None),
        P("strike", "cross", None),
        P("strike", "cross", None),
        P(),
        P("strike", "cross"),
        P("strike", "cross"),
        P("strike", "cross"),
        P("strike", "cross"),
    )
    out_specs = (
        P(None, "strike", "cross", None),
        P(None, "strike", "cross", None),
        P("strike", "cross"),
        P("strike", "cross"),
    )
    return jax.shard_map(local, mesh=mesh, in_specs=in_specs, out_specs=out_specs, check_vma=False)
```

```python
import functools

import jax
import jax.numpy as jnp
from jax import lax
from jax.experimental import pallas as pl
from jax.experimental.pallas import tpu as pltpu
from jax.sharding import PartitionSpec as P


STEPS = 4
NEWTON = 8

step_ratio = 0.25
ref_rate = 0.001
evolve_rate = 1e-05
base_friction = 0.6
evolve_b = 0.03
near_weight = 27.0
unit = step_ratio / 24.0

VMEM = pl.BlockSpec(memory_space=pltpu.VMEM)
SMEM = pl.BlockSpec(memory_space=pltpu.SMEM)
HBM = pl.BlockSpec(memory_space=pltpu.HBM)
PARAMS = pltpu.CompilerParams(vmem_limit_bytes=16 * 1024 * 1024)

STRESS_FACE = (((3, "b"), (4, "b"), (0, "f")), ((3, "b"), (5, "b"), (1, "f")))
VELOCITY_FACE = (((0, "b"), (1, "f"), (2, "f")), ((1, "b"), (0, "f"), (2, "f")))


def layers(kind):
    return (2, 1) if kind == "b" else (1, 2)


def combine(hi, lo, far_hi, far_lo):
    def sub(a, b):
        if a is None:
            return None if b is None else -b
        return a if b is None else a - b

    near, far = sub(hi, lo), sub(far_hi, far_lo)
    if near is None:
        return -far
    near = near_weight * near
    return near if far is None else near - far


def difference(kind, get):
    if kind == "b":
        return combine(get(0), get(-1), get(1), get(-2))
    return combine(get(1), get(0), get(2), get(-1))


def plane_shift(field, axis):
    length = field.shape[axis]
    place = lax.broadcasted_iota(jnp.int32, field.shape, axis)

    def get(k):
        if k == 0:
            return field
        rolled = pltpu.roll(field, (-k) % length, axis)
        keep = place < length - k if k > 0 else place >= -k
        return jnp.where(keep, rolled, 0.0)

    return get


def strike_shift(ref, comp, i, count):
    def get(k):
        return ref[comp, i + k] if 0 <= i + k < count else None

    return get


def add(*terms):
    return sum(terms[1:], terms[0])


def velocity_load_body(
    tile_ref, v_ref, s_ref, b_ref, out_ref, owner_ref, rows_ref, first_ref, sem, tile_smem, tile_sem
):
    groups = sem.shape[0]
    size = v_ref.shape[1] // groups
    parts = [(slice(None), pl.ds(g * size, size)) for g in range(groups)]
    copies = [
        pltpu.make_async_copy(v_ref.at[part], first_ref.at[part], sem.at[g])
        for g, part in enumerate(parts)
    ]
    tile_copy = pltpu.make_async_copy(tile_ref, tile_smem, tile_sem)
    for copy in (*copies, tile_copy):
        copy.start()
    for k, value in enumerate(edge_rows(b_ref, unit)):
        rows_ref[k] = value
    velocity_body(None, s_ref, b_ref, out_ref)
    tile_copy.wait()
    mine = tile_smem[lax.axis_index("strike")] == lax.axis_index("cross")
    owner_ref[...] = jnp.full(owner_ref.shape, mine.astype(jnp.float32))
    for copy, part in zip(copies, parts):
        copy.wait()
        out_ref[part] = out_ref[part] + first_ref[part]


def velocity_body(v_ref, s_ref, b_ref, out_ref):
    count = out_ref.shape[1]

    def store(comp, i, more):
        out_ref[comp, i] = more if v_ref is None else v_ref[comp, i] + more

    for i in range(count):
        gain = b_ref[i] * unit
        _, syy, szz, sxy, sxz, syz = (s_ref[c, i] for c in range(6))
        sxy_y, sxz_z = plane_shift(sxy, 0), plane_shift(sxz, 1)
        force = add(
            difference("f", strike_shift(s_ref, 0, i, count)),
            difference("b", sxy_y),
            difference("b", sxz_z),
        )
        store(0, i, gain * force)
        force = add(
            difference("b", strike_shift(s_ref, 3, i, count)),
            difference("f", plane_shift(syy, 0)),
            difference("b", plane_shift(syz, 1)),
        )
        store(1, i, gain * force)
        force = add(
            difference("b", strike_shift(s_ref, 4, i, count)),
            difference("b", plane_shift(syz, 0)),
            difference("f", plane_shift(szz, 1)),
        )
        store(2, i, gain * force)


def stress_store_body(s_ref, v_ref, lame_ref, shear_ref, out_ref, store_ref, sem):
    copy = pltpu.make_async_copy(v_ref, store_ref, sem)
    copy.start()
    stress_body(s_ref, v_ref, lame_ref, shear_ref, out_ref)
    copy.wait()


def stress_body(s_ref, v_ref, lame_ref, shear_ref, out_ref):
    count = s_ref.shape[1]
    for i in range(count):
        lam, mu = lame_ref[i] * unit, shear_ref[i] * unit
        vx, vy, vz = (v_ref[c, i] for c in range(3))
        ex = difference("b", strike_shift(v_ref, 0, i, count))
        ey = difference("b", plane_shift(vy, 0))
        ez = difference("b", plane_shift(vz, 1))
        spread = lam * (ex + ey + ez)
        twice = 2.0 * mu
        out_ref[0, i] = s_ref[0, i] + (spread + twice * ex)
        out_ref[1, i] = s_ref[1, i] + (spread + twice * ey)
        out_ref[2, i] = s_ref[2, i] + (spread + twice * ez)
        out_ref[3, i] = s_ref[3, i] + mu * (
            difference("f", plane_shift(vx, 0)) + difference("f", strike_shift(v_ref, 1, i, count))
        )
        out_ref[4, i] = s_ref[4, i] + mu * (
            difference("f", plane_shift(vx, 1)) + difference("f", strike_shift(v_ref, 2, i, count))
        )
        out_ref[5, i] = s_ref[5, i] + mu * (
            difference("f", plane_shift(vy, 1)) + difference("f", plane_shift(vz, 0))
        )


def row(axis, comp, i):
    return (comp, i) if axis == 0 else (comp, slice(None), i)


def slot(i, count):
    return i if i < 2 else i - count + 4


def edge_rows(ref, scale):
    count = ref.shape[1]
    return [ref[:, i] * scale for i in (0, 1, count - 2, count - 1)]


def side(axis):
    name = ("strike", "cross")[axis]
    pos, size = lax.axis_index(name), lax.axis_size(name)
    return lax.rem(pos, 2) == 0, pos > 0, pos < size - 1


def pack_steps(ref, axis, spec, a_ref, b_ref, rows=None):
    even, _, _ = side(axis)
    count = ref.shape[1 + axis]
    up, down = [], []
    for comp, kind in spec:
        before, after = layers(kind)
        up += [(comp, count - before + k) for k in range(before)]
        down += [(comp, k) for k in range(after)]

    def read(comp, i):
        if rows is not None:
            return rows[comp, i]
        return ref[row(axis, comp, i)]

    def step(k, first, second):
        high, low = read(*first), read(*second)
        a_ref[k] = lax.select(even, high, low)
        b_ref[k] = lax.select(even, low, high)

    for k in range(max(len(up), len(down))):
        first, second = up[min(k, len(up) - 1)], down[min(k, len(down) - 1)]
        yield (first, second), functools.partial(step, k, first, second)


def pack(*args):
    for _, step in pack_steps(*args):
        step()


def halo_terms(axis, spec, count, a_ref, b_ref):
    even, has_before, has_after = side(axis)
    terms = []
    at_before, at_after = 0, 0
    for comp, kind in spec:
        before, after = layers(kind)
        head, tail = [], []
        for k in range(before):
            j = at_before + k
            value = lax.select(even, b_ref[j], a_ref[j])
            head.append(lax.select(has_before, value, jnp.zeros_like(value)))
        for k in range(after):
            j = at_after + k
            value = lax.select(even, a_ref[j], b_ref[j])
            tail.append(lax.select(has_after, value, jnp.zeros_like(value)))
        at_before, at_after = at_before + before, at_after + after
        if kind == "b":
            update = {0: head[0] - near_weight * head[1], 1: head[1], count - 1: -tail[0]}
        else:
            update = {0: head[0], count - 2: -tail[0], count - 1: near_weight * tail[0] - tail[1]}
        terms.append(update)
    return terms


def grow(ref, at, more):
    value = ref[at] + more
    ref[at] = value
    return value


def velocity_edge_body(v_ref, b_ref, b_rows, xa, xb, ya, yb, out_ref, *packs):
    count = v_ref.shape[1]
    terms = halo_terms(0, STRESS_FACE[0], count, xa, xb)
    for target, update in zip((1, 2, 0), terms):
        for i, value in update.items():
            grow(out_ref, row(0, target, i), (b_ref[i] * unit) * value)
    count = v_ref.shape[2]
    terms = halo_terms(1, STRESS_FACE[1], count, ya, yb)
    rows = {}
    for target, update in zip((0, 2, 1), terms):
        for i, value in update.items():
            rows[target, i] = grow(out_ref, row(1, target, i), b_rows[slot(i, count)] * value)
    pack(out_ref, 1, VELOCITY_FACE[1], *packs[2:], rows)
    pack(out_ref, 0, VELOCITY_FACE[0], *packs[:2])


def velocity_ride_body(own_ref, v_ref, b_ref, b_rows, xa, xb, ya, yb, out_ref, *packs):
    velocity_edge_body(v_ref, b_ref, b_rows, xa, xb, ya, yb, out_ref, *packs)
    last = packs[3].shape[0] - 1
    packs[3][last - 1] = own_ref[...]
    packs[3][last] = ya[ya.shape[0] - 1]


def inverse_sinh(value):
    magnitude = jnp.abs(value)
    grown = jnp.log(magnitude + jnp.sqrt(magnitude * magnitude + 1.0))
    return jnp.where(value < 0.0, -grown, grown)


def friction(trial, damping, prestress, normal_stress, rate_a, state):
    total = trial + prestress
    width = 2.0 * ref_rate * jnp.exp(-state / rate_a)
    strength = rate_a * normal_stress
    drag = damping * width
    scaled = inverse_sinh(total / drag)
    yield
    for _ in range(NEWTON):
        grow, decay = 0.5 * jnp.exp(scaled), 0.5 * jnp.exp(-scaled)
        residual = strength * scaled + drag * (grow - decay) - total
        slope = strength + drag * (grow + decay)
        scaled = scaled - residual / slope
        yield
    slip = width * (0.5 * jnp.exp(scaled) - 0.5 * jnp.exp(-scaled))
    traction = total - damping * slip
    evolved = state + evolve_rate * (
        jnp.exp((base_friction - state) / evolve_b) - jnp.abs(slip) / ref_rate
    )
    yield (traction - prestress, slip, evolved)


def stress_edge_body(
    owner_ref, s_ref, lame_ref, shear_ref, material_rows, damping_ref, load_ref, normal_ref,
    rate_ref, state_ref, xa, xb, ya, yb, out_ref, *rest
):
    rows = {}
    counts = s_ref.shape[1:3]
    terms = [
        halo_terms(axis, VELOCITY_FACE[axis], counts[axis], a_ref, b_ref)
        for axis, a_ref, b_ref in ((0, xa, xb), (1, ya, yb))
    ]

    def material(axis, kind, i):
        if axis == 0:
            return (lame_ref, shear_ref)[kind][i] * unit
        return material_rows[4 * kind + slot(i, counts[axis])]

    def correct(axis, comp, i, more):
        value = grow(out_ref, row(axis, comp, i), more)
        if axis == 1:
            rows[comp, i] = value

    def tangent(axis, comp, i, value):
        correct(axis, comp, i, material(axis, 1, i) * value)

    def normal(axis, i, value):
        spread = material(axis, 0, i) * value
        for comp in range(3):
            more = spread + 2.0 * material(axis, 1, i) * value if comp == axis else spread
            correct(axis, comp, i, more)

    for i, value in terms[0][1].items():
        tangent(0, 3, i, value)
    tangent(1, 3, 0, terms[1][1].pop(0))
    trial = rows[3, 0]
    solve = friction(
        trial, damping_ref[...], load_ref[...], normal_ref[...], rate_ref[...], state_ref[...]
    )
    work = [functools.partial(tangent, 1, 3, i, value) for i, value in terms[1][1].items()]
    for axis, comp in ((0, 4), (1, 5)):
        work += [functools.partial(tangent, axis, comp, i, value) for i, value in terms[axis][2].items()]
    for axis in (0, 1):
        work += [functools.partial(normal, axis, i, value) for i, value in terms[axis][0].items()]
    after = []
    packs = rest[1:] if len(rest[-1].shape) == 3 else ()
    if packs:
        for axis, held in ((1, rows), (0, None)):
            for reads, step in pack_steps(
                out_ref, axis, STRESS_FACE[axis], *packs[2 * axis : 2 * axis + 2], held
            ):
                late = any(comp == 3 and (axis == 0 or i == 0) for comp, i in reads)
                (after if late else work).append(step)
    stages = NEWTON + 1
    for stage in range(stages):
        next(solve)
        for step in work[stage * len(work) // stages : (stage + 1) * len(work) // stages]:
            step()
    change, slip, evolved = next(solve)
    is_owner = owner_ref[...] > 0.5
    rows[3, 0] = jnp.where(is_owner, change, trial)
    out_ref[row(1, 3, 0)] = rows[3, 0]
    for step in after:
        step()
    if packs:
        rest[0][...] = evolved
    else:
        spread_out(jnp.where(is_owner, slip, 0.0), jnp.where(is_owner, evolved, 0.0), rest)


def spread_out(slip, evolved, sends):
    lanes = sends[0].shape[1]
    width, rows = slip.shape[1], lanes // 2
    place = lax.broadcasted_iota(jnp.int32, slip.shape, 1)
    me = lax.axis_index("cross")
    for r, send_ref in enumerate(sends):
        offset = (me ^ r) * rows
        head = pltpu.roll(slip, lax.rem(width - offset, width), 1)
        tail = pltpu.roll(evolved, lax.rem(width + rows - offset, width), 1)
        send_ref[...] = jnp.where(place < rows, head, tail)[:, :lanes]


def stress_rows_body(b_ref, lame_ref, shear_ref, rows_ref, damping_ref):
    for k, value in enumerate(edge_rows(lame_ref, unit) + edge_rows(shear_ref, unit)):
        rows_ref[k] = value
    damping_ref[...] = 0.5 * jnp.sqrt(shear_ref[:, 0] / b_ref[:, 0])


def join(pieces, width):
    rest = width - sum(p.shape[1] for p in pieces)
    if rest:
        pieces.append(jnp.zeros((pieces[0].shape[0], rest), pieces[0].dtype))
    return jnp.concatenate(pieces, axis=1)


def fault_body(order, *refs):
    arrays = 4
    blocks, outs = refs[:-arrays], refs[-arrays:]
    held = [block[...] for block in blocks]
    count, width = len(held), held[0].shape[1]
    depth = outs[0].shape[1]
    rows = depth // count
    holder = order(lax.axis_index("cross"))
    place = lax.broadcasted_iota(jnp.int32, held[0].shape, 1)
    whole = [jnp.zeros_like(held[0])] * arrays
    for q in range(count):
        value = held[0]
        for at, block in zip(holder[1:], held[1:]):
            value = lax.select(at == q, block, value)
        mine = (place >= q * rows) & (place < (q + 1) * rows)
        for k in range(arrays):
            shift = ((q - k) * rows) % width
            moved = pltpu.roll(value, shift, 1) if shift else value
            whole[k] = jnp.where(mine, moved, whole[k])
    for out_ref, value in zip(outs, whole):
        out_ref[...] = value[:, :depth]


def pack_body(s_ref, *rest):
    *sources, s_out, xa, xb, ya, yb, own_ref, part_ref, s_sem, part_sem = rest
    parts = [pltpu.make_async_copy(ref, part_ref.at[k], part_sem.at[k]) for k, ref in enumerate(sources)]
    loads = [pltpu.make_async_copy(s_ref.at[c], s_out.at[c], s_sem.at[c]) for c in range(s_ref.shape[0])]
    across, along = ([comp for comp, _ in STRESS_FACE[axis]] for axis in (1, 0))
    along = [comp for comp in along if comp not in across]
    others = [comp for comp in range(len(loads)) if comp not in across + along]
    for comp in across + along:
        loads[comp].start()
    for copy in parts:
        copy.start()
    for comp in others:
        loads[comp].start()
    for comp in across:
        loads[comp].wait()
    pack(s_out, 1, STRESS_FACE[1], ya, yb)
    for comp in along:
        loads[comp].wait()
    pack(s_out, 0, STRESS_FACE[0], xa, xb)
    for copy in parts:
        copy.wait()
    own = join([part_ref[k] for k in range(len(sources))], own_ref.shape[1])
    own_ref[...] = own
    if ya.shape[0] > yb.shape[0]:
        ya[ya.shape[0] - 1] = own
    for comp in others:
        loads[comp].wait()


def swaps(pairs):
    return [p for i, j in pairs for p in ((i, j), (j, i))]


def exchange_pairs(n_strike, n_cross):
    def at(s, c):
        return s * n_cross + c

    strike_a = [(at(s, c), at(s + 1, c)) for s in range(0, n_strike - 1, 2) for c in range(n_cross)]
    strike_b = [(at(s, c), at(s + 1, c)) for s in range(1, n_strike - 1, 2) for c in range(n_cross)]
    cross_a = [(at(s, c), at(s, c + 1)) for s in range(n_strike) for c in range(0, n_cross - 1, 2)]
    cross_b = [(at(s, c), at(s, c + 1)) for s in range(n_strike) for c in range(1, n_cross - 1, 2)]
    cross_ring = cross_b + [(at(s, 0), at(s, n_cross - 1)) for s in range(n_strike)]
    half = n_cross // 2
    for s in (0, n_strike - 1):
        strike_b += [(at(s, c), at(s, c + half)) for c in range(half)]
    for c in (0, n_cross - 1):
        cross_b += [(at(s, c), at(s + 1, c)) for s in range(0, n_strike - 1, 2)]
    return tuple(swaps(p) for p in (strike_a, strike_b, cross_a, cross_b, cross_ring))


def cycle_order(me):
    size = lax.axis_size("cross")
    far = lax.rem(me + jnp.where(lax.rem(me, 2) == 0, size - 1, 1), size)
    return [me, me ^ 1, far, far ^ 1]


def local(
    velocity, stress, buoyancy, lame, shear, fault_tile, prestress, normal_stress, rate_a, state
):
    n_strike, n_cross = lax.axis_size("strike"), lax.axis_size("cross")
    axes = ("strike", "cross")
    strike_a, strike_b, cross_a, cross_b, cross_ring = exchange_pairs(n_strike, n_cross)
    _, nx, ny, nz = velocity.shape
    bz = prestress.shape[1]
    f32 = jnp.float32
    thick = 5
    vec = lambda *shape: jax.ShapeDtypeStruct(shape, f32)
    faces = (vec(thick, ny, nz), vec(thick, ny, nz), vec(thick, nx, nz), vec(thick, nx, nz))
    like_v, like_s = pltpu.VMEM(velocity.shape, f32), pltpu.VMEM(stress.shape, f32)
    plane = vec(nx, nz)

    def call(body, ins, outs, specs=None, alias=None, scratch=()):
        return pl.pallas_call(
            body,
            in_specs=[VMEM] * len(ins) if specs is None else specs,
            out_specs=[HBM if getattr(o, "hbm", False) else VMEM for o in outs],
            out_shape=[o.shape if getattr(o, "hbm", False) else o for o in outs],
            input_output_aliases={} if alias is None else {alias: 0},
            compiler_params=PARAMS,
            scratch_shapes=scratch,
        )(*ins)

    def exchange(packs, wrap=False):
        perms = dict(xa=strike_a, xb=strike_b, ya=cross_a, yb=cross_ring if wrap else cross_b)
        halos = {}
        for name, block in reversed(tuple(zip(perms, packs))):
            halos[name] = lax.ppermute(block, axes, perms[name])
        return [halos[name] for name in perms]

    def partner(block, r):
        pairs = [(s * n_cross + c, s * n_cross + (c ^ r)) for s in range(n_strike) for c in range(n_cross)]
        return lax.ppermute(block, axes, pairs)

    ride = n_cross == 4
    width = max(nz, 4 * bz)
    params = (prestress, normal_stress, rate_a, state)
    outs = (like_s, *faces[:2], vec(thick + ride, nx, nz), faces[3], vec(nx, width))
    sources = [pltpu.with_memory_space_constraint(x, pltpu.HBM) for x in (stress, *params)]
    dma = pltpu.SemaphoreType.DMA
    stress, *packs, own = call(
        pack_body, sources, outs, [HBM] * 5,
        scratch=[pltpu.VMEM((4, nx, bz), f32), dma((stress.shape[0],)), dma((4,))],
    )
    for iteration in range(STEPS):
        first, last = iteration == 0, iteration == STEPS - 1
        halos = exchange(packs)
        if first:
            sources = [pltpu.with_memory_space_constraint(x, pltpu.HBM) for x in (fault_tile, velocity)]
            velocity, owner, b_rows = call(
                velocity_load_body, (*sources, stress, buoyancy),
                (like_v, plane, vec(4, nx, nz)), [HBM, HBM, VMEM, VMEM],
                scratch=[
                    pltpu.VMEM(velocity.shape, f32), dma((8,)), pltpu.SMEM(fault_tile.shape, jnp.int32), dma
                ],
            )
        else:
            (velocity,) = call(velocity_body, (velocity, stress, buoyancy), (like_v,), alias=0)
        if first and ride:
            velocity, *packs = call(
                velocity_ride_body, (own, velocity, buoyancy, b_rows, *halos),
                (like_v, *faces[:3], vec(thick + 2, nx, nz)), alias=1,
            )
            near = halos[2]
        else:
            velocity, *packs = call(
                velocity_edge_body, (velocity, buoyancy, b_rows, *halos), (like_v, *faces), alias=0,
            )
        halos = exchange(packs, wrap=first and ride)
        if first:
            rows, damping = call(stress_rows_body, (buoyancy, lame, shear), (vec(8, nx, nz), plane))
        body, outs, scratch = stress_body, (like_s,), ()
        if last:
            body, outs = stress_store_body, (like_s, Stored(vec(*velocity.shape)))
            scratch = [pltpu.SemaphoreType.DMA]
        stress, *stored = call(
            body, (stress, velocity, lame, shear), outs,
            alias=0, scratch=scratch,
        )
        if first:
            if ride:
                blocks, order = (own, near, halos[3]), cycle_order
                body = lambda own, near, far, *outs: fault_body(
                    order, own, near.at[thick], far.at[thick], far.at[thick + 1], *outs
                )
            else:
                blocks = [own] + [partner(own, r) for r in range(1, n_cross)]
                order = lambda me: [me ^ r for r in range(n_cross)]
                body = lambda *refs: fault_body(order, *refs)
            *fault, fault_state = call(body, blocks, (plane,) * 4)
        outs = (like_s,) + (vec(nx, 2 * bz),) * n_cross if last else (like_s, plane, *faces)
        stress, fault_state, *packs = call(
            stress_edge_body,
            (owner, stress, lame, shear, rows, damping, *fault, fault_state, *halos),
            outs, alias=1,
        )

    sends = [fault_state, *packs]
    result = sum([partner(sends[r], r) for r in range(1, n_cross)], sends[0])
    return (stored[0], stress, result[:, :bz], result[:, bz:])


class Stored:
    hbm = True

    def __init__(self, shape):
        self.shape = shape


def solution(mesh):
    in_specs = (
        P(None, "strike", "cross", None),
        P(None, "strike", "cross", None),
        P("strike", "cross", None),
        P("strike", "cross", None),
        P("strike", "cross", None),
        P(),
        P("strike", "cross"),
        P("strike", "cross"),
        P("strike", "cross"),
        P("strike", "cross"),
    )
    out_specs = (
        P(None, "strike", "cross", None),
        P(None, "strike", "cross", None),
        P("strike", "cross"),
        P("strike", "cross"),
    )
    return jax.shard_map(local, mesh=mesh, in_specs=in_specs, out_specs=out_specs, check_vma=False)
```
